32 devices in a mesh: parts: 2 (over y), walk: 4 (over z), slab: 2 (over x), row: 2 (over core).
Axes of the slice: x: 2, y: 2, z: 4, core: 2. Of those that a mesh axis runs over, the one named last changes fastest.
Arguments:
- walkers: bfloat16 [64, 1024, 256], P(('parts', 'walk'), ('slab', 'row')), parts along dimension 0
- trial_orbitals: bfloat16 [2048, 256], P(('parts', 'slab', 'row')), parts along dimension 0
- cholesky: bfloat16 [16, 256, 1024], P(('parts', 'slab', 'row')), parts along dimension 0, may hold values from -0.359375 to 0.359375
- branches: int32 [64], P('parts'), parts along dimension 0, may hold values from 0 to 31, as said below
- counts: int32 [8], P(('parts', 'walk')), parts along dimension 0, may hold values from 4 to 8, as said below
- field: float32 [64, 1024], P(('parts', 'walk'), ('slab', 'row')), parts along dimension 0, may hold values from 0.7 to 1.3
Outputs:
- force_bias: float32 [64, 8], P(('parts', 'walk'), ('slab', 'row')), parts along dimension 0
- exchange_energy: float32 [64, 8], P(('parts', 'walk'), ('slab', 'row')), parts along dimension 0
The draws below stay inside these ranges and needn't reach their ends.
There are 2 independent parts, one for each index of `parts`. The reference program is written for one: setup_inputs(seed, part) draws one part's arguments, and reference() takes and returns one part's arrays. A program takes and returns all parts, laid end to end along the dimension named above; each array names one. Nothing has to cross between parts.
Inputs may be any that keep to these rules, and one draw needn't show every extreme that they name: `branches`: the new walkers of one walk index copy at most 2 walkers from any one walk index, and some walk index gives exactly 2 to some walk index. `counts`: at least one walk index has all 8 alive; the alive ones are the first of its walkers.
All inputs are finite; a program needn't handle non-finite values. Where the reference program divides by a largest or mean magnitude, that divisor is 1e-20 or more.
Results may differ from the reference program's by a relative error of at most 0.0068.
Values may be sent and summed in bfloat16 or wider, within the bound.
A program may use at most 64 MiB of HBM per device.

```python
import math
import jax
import jax.numpy as jnp
from jax import lax

ORB = 1024
ELEC = 256
WALK_DEV = 8
ITERS = 10
WALKERS = 32
NCHOL = 8
SLOTS = 2


def joint_draw(key):
    folded = jax.random.fold_in(key, 101)
    key_orbitals = jax.random.fold_in(folded, 0)
    key_mixing = jax.random.fold_in(folded, 1)
    key_residue = jax.random.fold_in(folded, 3)
    orbitals = jax.random.normal(key_orbitals, (ORB, ELEC), jnp.float32) / math.sqrt(ORB)
    mixing = jnp.eye(ELEC, dtype=jnp.float32)[None] + 0.3 / math.sqrt(ELEC) * jax.random.normal(key_mixing, (WALKERS, ELEC, ELEC), jnp.float32)
    residue = 0.5 / math.sqrt(ORB) * jax.random.normal(key_residue, (WALKERS, ORB, ELEC), jnp.float32)
    walkers = jnp.einsum('mn,wnk->wmk', orbitals, mixing) + residue
    return (orbitals, walkers)


def draw_walkers(key, part):
    orbitals, walkers = joint_draw(key)
    return walkers.astype(jnp.bfloat16)


def draw_trial_orbitals(key, part):
    orbitals, walkers = joint_draw(key)
    return orbitals.astype(jnp.bfloat16)


def draw_branches(key, part):
    folded = jax.random.fold_in(key, 202)
    key_scores, key_favour, key_local = jax.random.split(folded, 3)
    walk_count = WALKERS // WALK_DEV
    capacity = SLOTS
    candidates = walk_count * capacity
    favour = jax.random.randint(key_favour, (walk_count,), 0, 4) * 1536
    scores = jax.random.randint(key_scores, (walk_count, candidates), 0, 4096) + jnp.repeat(favour, capacity)[None, :]
    scores = scores * candidates + jnp.arange(candidates, dtype=jnp.int32)[None, :]
    top_values, chosen = lax.top_k(scores, WALK_DEV)
    sender = chosen // capacity
    local_index = jax.random.randint(key_local, (walk_count, WALK_DEV), 0, WALK_DEV)
    return (sender * WALK_DEV + local_index).reshape(WALKERS).astype(jnp.int32)


def draw_counts(key, part):
    folded = jax.random.fold_in(key, 303)
    key_counts, key_fullest = jax.random.split(folded)
    walk_count = WALKERS // WALK_DEV
    living = jax.random.randint(key_counts, (walk_count,), WALK_DEV // 2, WALK_DEV + 1)
    fullest = jax.random.randint(key_fullest, (), 0, walk_count)
    return living.at[fullest].set(WALK_DEV).astype(jnp.int32)


def shard_levels(rng, shape, cuts, low, top_value):
    level, own = 1.0, jax.random.fold_in(rng, 6)
    for dim, shards_of in cuts:
        draws = jnp.exp(jax.random.uniform(jax.random.fold_in(own, dim), (shards_of,), jnp.float32, low / len(cuts), top_value / len(cuts)))
        level = level * jnp.repeat(draws, shape[dim] // shards_of).reshape([-1 if axis == dim else 1 for axis in range(len(shape))])
    return level


def noise(own_key, extent, spread, limit, shards=(), kind=jnp.bfloat16):
    level = shard_levels(own_key, extent, shards, -0.22, 0.18) if shards else 1.0
    result = jax.random.normal(own_key, extent, jnp.float32) * spread * level
    return jnp.minimum(jnp.maximum(result, -limit), limit).astype(kind)


def setup_inputs(seed: int = 0, part: int = 0) -> dict:
    splits = jax.random.split(jax.random.key(seed), 7)
    part_splits = jax.random.split(jax.random.fold_in(splits[6], part), 7)
    return {
        "walkers": draw_walkers(jax.random.fold_in(jax.random.fold_in(splits[6], part), 71), part),
        "trial_orbitals": draw_trial_orbitals(jax.random.fold_in(jax.random.fold_in(splits[6], part), 71), part),
        "cholesky": noise(part_splits[2], (NCHOL, ELEC, ORB), 0.06, 0.359375, ((0, 4),)),
        "branches": draw_branches(jax.random.fold_in(jax.random.fold_in(splits[6], part), 71), part),
        "counts": draw_counts(jax.random.fold_in(jax.random.fold_in(splits[6], part), 71), part),
        "field": jnp.clip(0.7 + 0.59999996 * jax.random.uniform(part_splits[5], (WALKERS, ORB), jnp.float32) ** shard_levels(part_splits[5], (WALKERS, ORB), ((0, 4), (1, 4)), -0.2, 0.2), 0.7, 1.3),
    }


HIGHEST = lax.Precision.HIGHEST


def newton_schulz(intersection):
    column_max = jnp.max(jnp.sum(jnp.abs(intersection), axis=0))
    row_max = jnp.max(jnp.sum(jnp.abs(intersection), axis=1))
    inverse = intersection.T / (column_max * row_max)
    twice_identity = 2.0 * jnp.eye(intersection.shape[0], dtype=intersection.dtype)
    for iteration in range(ITERS):
        inverse = jnp.dot(inverse, twice_identity - jnp.dot(intersection, inverse, precision=HIGHEST), precision=HIGHEST)
    return inverse


def reference(walkers, trial_orbitals, cholesky, branches, counts, field):
    vectors = cholesky.astype(jnp.float32)

    def per_walker(walker_index):
        source = walkers[branches[walker_index]]
        walker = (source.astype(jnp.float32) * field[walker_index][:, None]).astype(jnp.bfloat16)
        intersection = jnp.dot(trial_orbitals.T, walker, preferred_element_type=jnp.float32)
        inverse = newton_schulz(intersection).astype(jnp.bfloat16)
        green_half = jnp.dot(walker, inverse, preferred_element_type=jnp.float32).astype(jnp.bfloat16)
        contracted = jnp.einsum('gnm,mk->gnk', vectors, green_half.astype(jnp.float32), precision=HIGHEST)
        living = (walker_index % WALK_DEV < counts[walker_index // WALK_DEV]).astype(jnp.float32)
        force_bias = jnp.trace(contracted, axis1=1, axis2=2) * living
        exchange_energy = -0.5 * jnp.einsum('gnk,gkn->g', contracted, contracted, precision=HIGHEST) * living
        return force_bias, exchange_energy

    force_bias, exchange_energy = lax.map(per_walker, jnp.arange(WALKERS, dtype=jnp.int32))
    return force_bias, exchange_energy
```

```python
import functools

import jax
import jax.numpy as jnp
from jax import lax
from jax.experimental import pallas as pl
from jax.experimental.pallas import tpu as pltpu
from jax.sharding import PartitionSpec as P

ITERS = 10
MESH = pl.DeviceIdType.MESH


def split(x):
    high = x.astype(jnp.bfloat16)
    low = (x - high.astype(jnp.float32)).astype(jnp.bfloat16)
    return high, low


def dot(a, b):
    return jnp.dot(a, b, preferred_element_type=jnp.float32)


def dot3(a, b):
    ah, al = split(a)
    bh, bl = split(b)
    return dot(ah, bh) + (dot(ah, bl) + dot(al, bh))


def kernel(
    sizes, out_ref, trial_ref, chol_ref, field_ref, bias_ref, exch_ref,
    raw, trial, field, prop, half, inter, stack, inverse,
    z_send, z_recv, x_send, x_recv, c_send, c_recv, i_send, i_recv,
    tx_send, tx_recv, tc_send, tc_recv, fx_send, fx_recv, fc_send, fc_recv, own_sem,
):
    walks, slabs, cores, slots, local = sizes
    walk, slab, core = lax.axis_index("walk"), lax.axis_index("slab"), lax.axis_index("row")
    rows, electrons = trial_ref.shape[1], trial_ref.shape[0]
    vectors = chol_ref.shape[0] // electrons
    mine = slab * cores + core

    def slab_peer(step):
        return lax.rem(slab + step, slabs)

    def core_peer(step):
        return lax.rem(core + step, cores)

    def slab_source(step):
        return lax.rem(slab + slabs - step, slabs)

    def core_source(step):
        return lax.rem(core + cores - step, cores)

    barrier = pltpu.get_barrier_semaphore()
    greeted = 0
    if local < slots:
        for step in range(1, walks):
            pl.semaphore_signal(barrier, inc=1, device_id={"walk": lax.rem(walk + step, walks)}, device_id_type=MESH)
            greeted += 1
    for step in range(1, slabs):
        pl.semaphore_signal(barrier, inc=1, device_id={"slab": slab_peer(step)}, device_id_type=MESH)
        greeted += 1
    for step in range(1, cores):
        pl.semaphore_signal(barrier, inc=1, device_id={"row": core_peer(step)}, device_id_type=MESH)
        greeted += 1
    pl.semaphore_wait(barrier, greeted)

    def remote(src, dst, send, recv, target):
        return pltpu.make_async_remote_copy(
            src_ref=src, dst_ref=dst, send_sem=send, recv_sem=recv, device_id=target, device_id_type=MESH
        )

    def z_copy(i, step):
        return remote(out_ref.at[i], raw.at[i, mine], z_send.at[i], z_recv.at[i], {"walk": lax.rem(walk + step, walks)})

    def x_copy(i, step):
        return remote(raw.at[i, mine], raw.at[i, mine], x_send.at[step, i], x_recv.at[step, i], {"slab": slab_peer(step)})

    def c_copy(i, hop, step):
        q = slab_source(hop) * cores + core
        return remote(raw.at[i, q], raw.at[i, q], c_send.at[hop, step, i], c_recv.at[hop, step, i], {"row": core_peer(step)})

    def small(src, buf, xs, xr, cs, cr):
        def x(step):
            return remote(src, buf.at[mine], xs.at[step], xr.at[step], {"slab": slab_peer(step)})

        def c(hop, step):
            q = slab_source(hop) * cores + core
            block = src if hop == 0 else buf.at[q]
            return remote(block, buf.at[q], cs.at[hop, step], cr.at[hop, step], {"row": core_peer(step)})

        return x, c

    own = [pltpu.make_async_copy(out_ref.at[i], raw.at[i, mine], own_sem.at[i]) for i in range(local)]
    own.append(pltpu.make_async_copy(trial_ref, trial.at[mine], own_sem.at[local]))
    own.append(pltpu.make_async_copy(field_ref, field.at[mine], own_sem.at[local + 1]))
    for copy in own:
        copy.start()
    for i in range(local, slots):
        z_copy(i, i // local).start()
    pairs = [
        small(trial_ref, trial, tx_send, tx_recv, tc_send, tc_recv),
        small(field_ref, field, fx_send, fx_recv, fc_send, fc_recv),
    ]
    for x, c in pairs:
        for step in range(1, slabs):
            x(step).start()
        for step in range(1, cores):
            c(0, step).start()
    for copy in own:
        copy.wait()

    def spread(i):
        for step in range(1, slabs):
            x_copy(i, step).start()
        for step in range(1, cores):
            c_copy(i, 0, step).start()

    def relay(i):
        for hop in range(1, slabs):
            x_copy(i, hop).wait_recv()
            for step in range(1, cores):
                c_copy(i, hop, step).start()

    def compute(i):
        for hop in range(slabs):
            for step in range(1, cores):
                c_copy(i, hop, step).wait_recv()
        for q in range(slabs * cores):
            column = jnp.transpose(field[q])
            lane = lax.broadcasted_iota(jnp.int32, column.shape, 1)
            scale = jnp.sum(jnp.where(lane == i, column, 0.0), axis=1, keepdims=True)
            prop[q * rows : (q + 1) * rows, :] = (raw[i, q].astype(jnp.float32) * scale).astype(jnp.bfloat16)
        half[i] = dot(chol_ref[...], prop[...]).astype(jnp.bfloat16)

        @pl.when(lax.rem(i, cores) == core)
        def _():
            total = dot(trial[0], prop[0:rows, :])
            for q in range(1, slabs * cores):
                total += dot(trial[q], prop[q * rows : (q + 1) * rows, :])
            inter[i // cores] = total

    for i in range(local):
        spread(i)
    for x, c in pairs:
        for hop in range(1, slabs):
            x(hop).wait_recv()
            for step in range(1, cores):
                c(hop, step).start()
    for x, c in pairs:
        for hop in range(slabs):
            for step in range(1, cores):
                c(hop, step).wait_recv()

    @pl.loop(0, slots + 2)
    def _(i):
        @pl.when((i >= local) & (i < slots))
        def _():
            z_copy(i, 0).wait_recv()
            spread(i)

        @pl.when((i > 0) & (i <= slots))
        def _():
            relay(i - 1)

        @pl.when(i > 1)
        def _():
            compute(i - 2)

    share = slots // cores
    for n in range(share):
        matrix = inter[n]
        sizes_of = jnp.abs(matrix)
        column_max = jnp.max(jnp.sum(sizes_of, axis=0, keepdims=True), axis=1, keepdims=True)
        row_max = jnp.max(jnp.sum(sizes_of, axis=1, keepdims=True), axis=0, keepdims=True)
        start = jnp.transpose(matrix) / (column_max * row_max)
        stack[n, 0:electrons, :] = start
        stack[n, electrons:, :] = dot3(matrix, start)

    @pl.loop(0, ITERS)
    def _(iteration):
        for n in range(share):
            both = stack[n]
            stack[n] = 2.0 * both - dot3(both, both[electrons:, :])

    def i_copy(n, c, step):
        place = inverse.at[n * cores + c]
        return remote(place, place, i_send.at[n, step], i_recv.at[n, step], {"row": core_peer(step)})

    for n in range(share):
        inverse[n * cores + core] = stack[n, 0:electrons, :].astype(jnp.bfloat16)
        for step in range(1, cores):
            i_copy(n, core, step).start()
    for n in range(share):
        for step in range(1, cores):
            i_copy(n, core_source(step), step).wait_recv()

    line = lax.broadcasted_iota(jnp.int32, (electrons, electrons), 0)
    diagonal = line == lax.broadcasted_iota(jnp.int32, (electrons, electrons), 1)

    @pl.loop(0, slots)
    def _(i):
        contracted = dot(half[i], inverse[i])
        for g in range(vectors):
            block = contracted[g * electrons : (g + 1) * electrons, :]
            bias_ref[i, g : g + 1, :] = jnp.sum(jnp.where(diagonal, block, 0.0), axis=0, keepdims=True)
            exch_ref[i, g : g + 1, :] = jnp.sum(block * jnp.transpose(block), axis=0, keepdims=True)

    for i in range(local, slots):
        z_copy(i, i // local).wait_send()

    @pl.loop(0, slots)
    def _(i):
        for step in range(1, slabs):
            x_copy(i, step).wait_send()
        for hop in range(slabs):
            for step in range(1, cores):
                c_copy(i, hop, step).wait_send()

    for x, c in pairs:
        for step in range(1, slabs):
            x(step).wait_send()
        for hop in range(slabs):
            for step in range(1, cores):
                c(hop, step).wait_send()
    for n in range(share):
        for step in range(1, cores):
            i_copy(n, core, step).wait_send()


def on_device(walkers, trial_orbitals, cholesky, branches, counts, field):
    walks, slabs, cores = lax.axis_size("walk"), lax.axis_size("slab"), lax.axis_size("row")
    walk = lax.axis_index("walk")
    per_device, rows, electrons = walkers.shape
    vectors = cholesky.shape[0]
    capacity = (per_device + walks - 1) // walks
    sender = branches.reshape(walks, per_device) // per_device
    local_index = branches.reshape(walks, per_device) % per_device
    places = jnp.arange(per_device, dtype=jnp.int32)
    same_sender = sender[:, :, None] == sender[:, None, :]
    rank = jnp.sum(same_sender & (places[None, :] < places[:, None])[None], axis=2)
    my_sender = lax.dynamic_index_in_dim(sender, walk, 0, keepdims=False)
    my_rank = lax.dynamic_index_in_dim(rank, walk, 0, keepdims=False)
    full = walks * capacity == per_device
    wanted = (sender[:, None, :] == walk) & (rank[:, None, :] == jnp.arange(capacity, dtype=jnp.int32)[None, :, None])
    chosen = jnp.sum(jnp.where(wanted, local_index[:, None, :], 0), axis=2)
    if full:
        steps = jnp.arange(walks, dtype=jnp.int32)
        order = (walk + steps) % walks
        chosen = jnp.sum(jnp.where(order[:, None, None] == steps[None, :, None], chosen[None], 0), axis=1)
        outgoing = jnp.take(walkers, chosen.reshape(-1), axis=0, mode="clip")
        slot = ((walk - my_sender) % walks) * capacity + my_rank
        local = capacity
    else:
        outgoing = jnp.take(walkers, chosen.reshape(-1), axis=0, mode="clip")
        outgoing = outgoing.reshape(walks, capacity, rows, electrons)
        arrived = lax.all_to_all(outgoing, "walk", split_axis=0, concat_axis=0, tiled=True)
        arrived = arrived.reshape(walks * capacity, rows, electrons)
        outgoing = jnp.take(arrived, my_sender * capacity + my_rank, axis=0, mode="clip")
        slot = places
        local = per_device
    here = slot[:, None] == places[None, :]
    slot_field = jnp.sum(jnp.where(here[:, :, None], field[:, None, :], 0.0), axis=0)
    shards = slabs * cores
    share = per_device // cores
    dma = pltpu.SemaphoreType.DMA
    vmem = pl.BlockSpec(memory_space=pltpu.VMEM)
    bias, exchange = pl.pallas_call(
        functools.partial(kernel, (walks, slabs, cores, per_device, local)),
        out_shape=[jax.ShapeDtypeStruct((per_device, vectors, electrons), jnp.float32)] * 2,
        in_specs=[vmem] * 4,
        out_specs=[vmem] * 2,
        scratch_shapes=[
            pltpu.VMEM((per_device, shards, rows, electrons), jnp.bfloat16),
            pltpu.VMEM((shards, electrons, rows), jnp.bfloat16),
            pltpu.VMEM((shards, per_device, rows), jnp.float32),
            pltpu.VMEM((shards * rows, electrons), jnp.bfloat16),
            pltpu.VMEM((per_device, vectors * electrons, electrons), jnp.bfloat16),
            pltpu.VMEM((share, electrons, electrons), jnp.float32),
            pltpu.VMEM((share, 2 * electrons, electrons), jnp.float32),
            pltpu.VMEM((per_device, electrons, electrons), jnp.bfloat16),
            dma((per_device,)), dma((per_device,)),
            dma((slabs, per_device)), dma((slabs, per_device)),
            dma((slabs, cores, per_device)), dma((slabs, cores, per_device)),
            dma((share, cores)), dma((share, cores)),
            dma((slabs,)), dma((slabs,)), dma((slabs, cores)), dma((slabs, cores)),
            dma((slabs,)), dma((slabs,)), dma((slabs, cores)), dma((slabs, cores)),
            dma((local + 2,)),
        ],
        compiler_params=pltpu.CompilerParams(
            collective_id=0, has_side_effects=True, vmem_limit_bytes=48 * 1024 * 1024
        ),
    )(outgoing, trial_orbitals.T, cholesky.reshape(vectors * electrons, shards * rows), slot_field)
    living = (places < counts[0]).astype(jnp.float32)[:, None]
    bias = jnp.sum(jnp.where(here[:, :, None], jnp.sum(bias, axis=2)[None], 0.0), axis=1)
    exchange = jnp.sum(jnp.where(here[:, :, None], jnp.sum(exchange, axis=2)[None], 0.0), axis=1)
    return bias * living, -0.5 * exchange * living


def solution(mesh):
    return jax.shard_map(
        on_device,
        mesh=mesh,
        in_specs=(
            P(("parts", "walk"), ("slab", "row"), None),
            P(("parts", "slab", "row"), None),
            P(("parts", "slab", "row"), None, None),
            P("parts"),
            P(("parts", "walk")),
            P(("parts", "walk"), ("slab", "row")),
        ),
        out_specs=(P(("parts", "walk"), ("slab", "row")), P(("parts", "walk"), ("slab", "row"))),
        check_vma=False,
    )
```

```python
import functools

import jax
import jax.numpy as jnp
from jax import lax
from jax.experimental import pallas as pl
from jax.experimental.pallas import tpu as pltpu
from jax.sharding import PartitionSpec as P

ITERS = 10
MESH = pl.DeviceIdType.MESH


def split(x):
    high = x.astype(jnp.bfloat16)
    low = (x - high.astype(jnp.float32)).astype(jnp.bfloat16)
    return high, low


def dot(a, b):
    return jnp.dot(a, b, preferred_element_type=jnp.float32)


def dot3(a, b):
    ah, al = split(a)
    bh, bl = split(b)
    return dot(ah, bh) + (dot(ah, bl) + dot(al, bh))


def partner(position, step, size):
    if size & (size - 1):
        return (position + step) % size
    result, bit = 0, 1
    while bit < size:
        digit = (position // bit) % 2
        result += bit * (1 - digit if step & bit else digit)
        bit *= 2
    return result


def kernel(
    sizes, out_ref, trial_ref, chol_ref, field_ref, bias_ref, exch_ref,
    raw, trial, field, chol, prop, half, inter, stack, inverse,
    z_send, z_recv, x_send, x_recv, c_send, c_recv, i_send, i_recv,
    tx_send, tx_recv, tc_send, tc_recv, fx_send, fx_recv, fc_send, fc_recv, own_sem,
):
    walks, slabs, cores, slots, local = sizes
    walk, slab, core = lax.axis_index("walk"), lax.axis_index("slab"), lax.axis_index("row")
    rows, electrons = trial_ref.shape[1], trial_ref.shape[0]
    vectors = chol_ref.shape[0] // electrons
    mine = slab * cores + core

    def slab_peer(step):
        return lax.rem(slab + step, slabs)

    def core_peer(step):
        return lax.rem(core + step, cores)

    def slab_source(step):
        return lax.rem(slab + slabs - step, slabs)

    def core_source(step):
        return lax.rem(core + cores - step, cores)

    own = [pltpu.make_async_copy(out_ref.at[i], raw.at[i, mine], own_sem.at[i]) for i in range(local)]
    own.append(pltpu.make_async_copy(trial_ref, trial.at[mine], own_sem.at[local]))
    own.append(pltpu.make_async_copy(field_ref, field.at[mine], own_sem.at[local + 1]))
    own.append(pltpu.make_async_copy(chol_ref, chol, own_sem.at[local + 2]))
    for copy in own:
        copy.start()
    barrier = pltpu.get_barrier_semaphore()
    greeted = 0
    if local < slots:
        for step in range(1, walks):
            pl.semaphore_signal(barrier, inc=1, device_id={"walk": partner(walk, step, walks)}, device_id_type=MESH)
            greeted += 1
    for step in range(1, slabs):
        pl.semaphore_signal(barrier, inc=1, device_id={"slab": slab_peer(step)}, device_id_type=MESH)
        greeted += 1
    for step in range(1, cores):
        pl.semaphore_signal(barrier, inc=1, device_id={"row": core_peer(step)}, device_id_type=MESH)
        greeted += 1
    pl.semaphore_wait(barrier, greeted)

    def remote(src, dst, send, recv, target):
        return pltpu.make_async_remote_copy(
            src_ref=src, dst_ref=dst, send_sem=send, recv_sem=recv, device_id=target, device_id_type=MESH
        )

    def z_copy(i, step):
        return remote(out_ref.at[i], raw.at[i, mine], z_send.at[i], z_recv.at[i], {"walk": partner(walk, step, walks)})

    def x_copy(i, step):
        return remote(raw.at[i, mine], raw.at[i, mine], x_send.at[step, i], x_recv.at[step, i], {"slab": slab_peer(step)})

    def c_copy(i, hop, step):
        q = slab_source(hop) * cores + core
        return remote(raw.at[i, q], raw.at[i, q], c_send.at[hop, step, i], c_recv.at[hop, step, i], {"row": core_peer(step)})

    def small(src, buf, xs, xr, cs, cr):
        def x(step):
            return remote(src, buf.at[mine], xs.at[step], xr.at[step], {"slab": slab_peer(step)})

        def c(hop, step):
            q = slab_source(hop) * cores + core
            block = src if hop == 0 else buf.at[q]
            return remote(block, buf.at[q], cs.at[hop, step], cr.at[hop, step], {"row": core_peer(step)})

        return x, c

    for i in range(local, slots):
        z_copy(i, i // local).start()
    pairs = [
        small(trial_ref, trial, tx_send, tx_recv, tc_send, tc_recv),
        small(field_ref, field, fx_send, fx_recv, fc_send, fc_recv),
    ]
    for x, c in pairs:
        for step in range(1, slabs):
            x(step).start()
        for step in range(1, cores):
            c(0, step).start()
    for copy in own:
        copy.wait()

    def spread(i):
        for step in range(1, slabs):
            x_copy(i, step).start()
        for step in range(1, cores):
            c_copy(i, 0, step).start()

    def relay(i):
        for hop in range(1, slabs):
            x_copy(i, hop).wait_recv()
            for step in range(1, cores):
                c_copy(i, hop, step).start()

    def compute(i):
        for hop in range(slabs):
            for step in range(1, cores):
                c_copy(i, hop, step).wait_recv()
        for q in range(slabs * cores):
            column = jnp.transpose(field[q])
            lane = lax.broadcasted_iota(jnp.int32, column.shape, 1)
            scale = jnp.sum(jnp.where(lane == i, column, 0.0), axis=1, keepdims=True)
            prop[q * rows : (q + 1) * rows, :] = (raw[i, q].astype(jnp.float32) * scale).astype(jnp.bfloat16)
        half[i] = dot(chol[...], prop[...]).astype(jnp.bfloat16)

        @pl.when(lax.rem(i, cores) == core)
        def _():
            total = dot(trial[0], prop[0:rows, :])
            for q in range(1, slabs * cores):
                total += dot(trial[q], prop[q * rows : (q + 1) * rows, :])
            inter[i // cores] = total

    for i in range(local):
        spread(i)
    for x, c in pairs:
        for hop in range(1, slabs):
            x(hop).wait_recv()
            for step in range(1, cores):
                c(hop, step).start()
    for x, c in pairs:
        for hop in range(slabs):
            for step in range(1, cores):
                c(hop, step).wait_recv()

    share = slots // cores
    line = lax.broadcasted_iota(jnp.int32, (electrons, electrons), 0)
    diagonal = line == lax.broadcasted_iota(jnp.int32, (electrons, electrons), 1)

    def i_copy(i, step):
        place = inverse.at[i]
        return remote(place, place, i_send.at[i // cores, step], i_recv.at[i // cores, step], {"row": core_peer(step)})

    def first_guess(n):
        matrix = inter[n]
        sizes_of = jnp.abs(matrix)
        column_max = jnp.max(jnp.sum(sizes_of, axis=0, keepdims=True), axis=1, keepdims=True)
        row_max = jnp.max(jnp.sum(sizes_of, axis=1, keepdims=True), axis=0, keepdims=True)
        start = jnp.transpose(matrix) / (column_max * row_max)
        stack[0:electrons, :] = start
        stack[electrons:, :] = dot3(matrix, start)

    def finish(i):
        @pl.when(lax.rem(i, cores) != core)
        def _():
            i_copy(i, lax.rem(core + cores - lax.rem(i, cores), cores)).wait_recv()

        contracted = dot(half[i], inverse[i])
        for g in range(vectors):
            block = contracted[g * electrons : (g + 1) * electrons, :]
            bias_ref[i, g : g + 1, :] = jnp.sum(jnp.where(diagonal, block, 0.0), axis=0, keepdims=True)
            exch_ref[i, g : g + 1, :] = jnp.sum(block * jnp.transpose(block), axis=0, keepdims=True)

    ready = cores + 1

    @pl.loop(0, slots + ready + cores)
    def _(i):
        @pl.when((i >= local) & (i < slots))
        def _():
            z_copy(i, 0).wait_recv()
            spread(i)

        @pl.when((i > 0) & (i <= slots))
        def _():
            relay(i - 1)

        @pl.when((i > 1) & (i < slots + 2))
        def _():
            compute(i - 2)

        for part in range(cores):

            @pl.when((i >= ready) & (i < slots + ready) & (lax.rem(i + cores - 1, cores) == part))
            def _():
                n = (i - ready) // cores
                if part == 0:
                    first_guess(n)

                @pl.loop(ITERS * part // cores, ITERS * (part + 1) // cores)
                def _(iteration):
                    both = stack[...]
                    stack[...] = 2.0 * both - dot3(both, both[electrons:, :])

                if part == cores - 1:
                    inverse[n * cores + core] = stack[0:electrons, :].astype(jnp.bfloat16)
                    for step in range(1, cores):
                        i_copy(n * cores + core, step).start()

        @pl.when(i >= ready + cores)
        def _():
            finish(i - ready - cores)

    for i in range(local, slots):
        z_copy(i, i // local).wait_send()

    @pl.loop(0, slots)
    def _(i):
        for step in range(1, slabs):
            x_copy(i, step).wait_send()
        for hop in range(slabs):
            for step in range(1, cores):
                c_copy(i, hop, step).wait_send()

    for x, c in pairs:
        for step in range(1, slabs):
            x(step).wait_send()
        for hop in range(slabs):
            for step in range(1, cores):
                c(hop, step).wait_send()
    for n in range(share):
        for step in range(1, cores):
            i_copy(n * cores + core, step).wait_send()


def on_device(walkers, trial_orbitals, cholesky, branches, counts, field):
    walks, slabs, cores = lax.axis_size("walk"), lax.axis_size("slab"), lax.axis_size("row")
    walk = lax.axis_index("walk")
    per_device, rows, electrons = walkers.shape
    vectors = cholesky.shape[0]
    capacity = (per_device + walks - 1) // walks
    sender = branches.reshape(walks, per_device) // per_device
    local_index = branches.reshape(walks, per_device) % per_device
    places = jnp.arange(per_device, dtype=jnp.int32)
    same_sender = sender[:, :, None] == sender[:, None, :]
    rank = jnp.sum(same_sender & (places[None, :] < places[:, None])[None], axis=2)
    my_sender = lax.dynamic_index_in_dim(sender, walk, 0, keepdims=False)
    my_rank = lax.dynamic_index_in_dim(rank, walk, 0, keepdims=False)
    full = walks * capacity == per_device
    wanted = (sender[:, None, :] == walk) & (rank[:, None, :] == jnp.arange(capacity, dtype=jnp.int32)[None, :, None])
    chosen = jnp.sum(jnp.where(wanted, local_index[:, None, :], 0), axis=2)
    if full:
        steps = jnp.arange(walks, dtype=jnp.int32)
        order = jnp.stack([partner(walk, step, walks) for step in range(walks)])
        origin = order if walks & (walks - 1) == 0 else (walk - steps) % walks
        chosen = jnp.sum(jnp.where(order[:, None, None] == steps[None, :, None], chosen[None], 0), axis=1)
        outgoing = jnp.take(walkers, chosen.reshape(-1), axis=0, mode="clip")
        step_of = jnp.sum(jnp.where(my_sender[:, None] == origin[None, :], steps[None, :], 0), axis=1)
        slot = step_of * capacity + my_rank
        local = capacity
    else:
        outgoing = jnp.take(walkers, chosen.reshape(-1), axis=0, mode="clip")
        outgoing = outgoing.reshape(walks, capacity, rows, electrons)
        arrived = lax.all_to_all(outgoing, "walk", split_axis=0, concat_axis=0, tiled=True)
        arrived = arrived.reshape(walks * capacity, rows, electrons)
        outgoing = jnp.take(arrived, my_sender * capacity + my_rank, axis=0, mode="clip")
        slot = places
        local = per_device
    here = slot[:, None] == places[None, :]
    slot_field = jnp.sum(jnp.where(here[:, :, None], field[:, None, :], 0.0), axis=0)
    shards = slabs * cores
    share = per_device // cores
    dma = pltpu.SemaphoreType.DMA
    vmem = pl.BlockSpec(memory_space=pltpu.VMEM)
    bias, exchange = pl.pallas_call(
        functools.partial(kernel, (walks, slabs, cores, per_device, local)),
        out_shape=[jax.ShapeDtypeStruct((per_device, vectors, electrons), jnp.float32)] * 2,
        in_specs=[pl.BlockSpec(memory_space=pl.ANY)] * 4,
        out_specs=[vmem] * 2,
        scratch_shapes=[
            pltpu.VMEM((per_device, shards, rows, electrons), jnp.bfloat16),
            pltpu.VMEM((shards, electrons, rows), jnp.bfloat16),
            pltpu.VMEM((shards, per_device, rows), jnp.float32),
            pltpu.VMEM((vectors * electrons, shards * rows), jnp.bfloat16),
            pltpu.VMEM((shards * rows, electrons), jnp.bfloat16),
            pltpu.VMEM((per_device, vectors * electrons, electrons), jnp.bfloat16),
            pltpu.VMEM((share, electrons, electrons), jnp.float32),
            pltpu.VMEM((2 * electrons, electrons), jnp.float32),
            pltpu.VMEM((per_device, electrons, electrons), jnp.bfloat16),
            dma((per_device,)), dma((per_device,)),
            dma((slabs, per_device)), dma((slabs, per_device)),
            dma((slabs, cores, per_device)), dma((slabs, cores, per_device)),
            dma((share, cores)), dma((share, cores)),
            dma((slabs,)), dma((slabs,)), dma((slabs, cores)), dma((slabs, cores)),
            dma((slabs,)), dma((slabs,)), dma((slabs, cores)), dma((slabs, cores)),
            dma((local + 3,)),
        ],
        compiler_params=pltpu.CompilerParams(
            collective_id=0, has_side_effects=True, vmem_limit_bytes=48 * 1024 * 1024
        ),
    )(outgoing, trial_orbitals.T, cholesky.reshape(vectors * electrons, shards * rows), slot_field)
    living = (places < counts[0]).astype(jnp.float32)[:, None]
    bias = jnp.sum(jnp.where(here[:, :, None], jnp.sum(bias, axis=2)[None], 0.0), axis=1)
    exchange = jnp.sum(jnp.where(here[:, :, None], jnp.sum(exchange, axis=2)[None], 0.0), axis=1)
    return bias * living, -0.5 * exchange * living


def solution(mesh):
    return jax.shard_map(
        on_device,
        mesh=mesh,
        in_specs=(
            P(("parts", "walk"), ("slab", "row"), None),
            P(("parts", "slab", "row"), None),
            P(("parts", "slab", "row"), None, None),
            P("parts"),
            P(("parts", "walk")),
            P(("parts", "walk"), ("slab", "row")),
        ),
        out_specs=(P(("parts", "walk"), ("slab", "row")), P(("parts", "walk"), ("slab", "row"))),
        check_vma=False,
    )
```

```python
import functools

import jax
import jax.numpy as jnp
from jax import lax
from jax.experimental import pallas as pl
from jax.experimental.pallas import tpu as pltpu
from jax.sharding import PartitionSpec as P

ITERS = 10
EARLY = 4
MESH = pl.DeviceIdType.MESH


def split(x):
    high = x.astype(jnp.bfloat16)
    low = (x - high.astype(jnp.float32)).astype(jnp.bfloat16)
    return high, low


def dot(a, b):
    return jnp.dot(a, b, preferred_element_type=jnp.float32)


def dot3(a, b):
    ah, al = split(a)
    bh, bl = split(b)
    return dot(ah, bh) + (dot(ah, bl) + dot(al, bh))


def partner(position, step, size):
    if size & (size - 1):
        return (position + step) % size
    result, bit = 0, 1
    while bit < size:
        digit = (position // bit) % 2
        result += bit * (1 - digit if step & bit else digit)
        bit *= 2
    return result


def kernel(
    sizes, branch_ref, count_ref, walker_ref, trial_ref, chol_ref, field_ref, bias_ref, exch_ref,
    source, outgoing, field_in, field_out, traces, squares, bias_rows, exch_rows, raw, trial, field, chol, prop, half, inter, stack, inverse,
    z_send, z_recv, x_send, x_recv, c_send, c_recv, i_send, i_recv,
    tx_send, tx_recv, tc_send, tc_recv, fx_send, fx_recv, fc_send, fc_recv, own_sem,
):
    walks, slabs, cores, slots, local = sizes
    walk, slab, core = lax.axis_index("walk"), lax.axis_index("slab"), lax.axis_index("row")
    rows, electrons = trial_ref.shape[1], trial_ref.shape[0]
    vectors = chol_ref.shape[0] // electrons
    mine = slab * cores + core

    def slab_peer(step):
        return lax.rem(slab + step, slabs)

    def core_peer(step):
        return lax.rem(core + step, cores)

    def slab_source(step):
        return lax.rem(slab + slabs - step, slabs)

    def core_source(step):
        return lax.rem(core + cores - step, cores)

    loads = [(walker_ref, source), (field_ref, field_in), (trial_ref, trial.at[mine]), (chol_ref, chol)]
    own = [pltpu.make_async_copy(src, dst, own_sem.at[k]) for k, (src, dst) in enumerate(loads)]
    for copy in own:
        copy.start()
    barrier = pltpu.get_barrier_semaphore()
    greeted = 0
    if local < slots:
        for step in range(1, walks):
            pl.semaphore_signal(barrier, inc=1, device_id={"walk": partner(walk, step, walks)}, device_id_type=MESH)
            greeted += 1
    for step in range(1, slabs):
        pl.semaphore_signal(barrier, inc=1, device_id={"slab": slab_peer(step)}, device_id_type=MESH)
        greeted += 1
    for step in range(1, cores):
        pl.semaphore_signal(barrier, inc=1, device_id={"row": core_peer(step)}, device_id_type=MESH)
        greeted += 1

    def sender(w, k):
        return lax.div(branch_ref[w * slots + k], slots)

    def kth(w, origin, values):
        picks, count = [jnp.int32(0)] * local, jnp.int32(0)
        for k in range(slots):
            hit = sender(w, k) == origin
            picks = [jnp.where(hit & (count == place), values(k), pick) for place, pick in enumerate(picks)]
            count = count + jnp.where(hit, 1, 0)
        return picks

    for copy in own[:2]:
        copy.wait()
    slot_of = list(range(slots))
    if local < slots:
        origins = []
        for step in range(walks):
            target = partner(walk, step, walks)
            picks = kth(target, walk, lambda k: lax.rem(branch_ref[target * slots + k], slots))
            for place, pick in enumerate(picks):
                if step == 0:
                    raw[place, mine] = source[pick]
                else:
                    outgoing[step * local + place] = source[pick]
            origin = target if walks & (walks - 1) == 0 else (walk + walks - step) % walks
            origins.append(origin)
            for place, pick in enumerate(kth(walk, origin, lambda k: k)):
                i = step * local + place
                field_out[i : i + 1, :] = field_in[pl.ds(pick, 1), :]
        for j in range(slots):
            origin, rank, step_of = sender(walk, j), jnp.int32(0), jnp.int32(0)
            for k in range(j):
                rank = rank + jnp.where(sender(walk, k) == origin, 1, 0)
            for step in range(walks):
                step_of = jnp.where(origins[step] == origin, step, step_of)
            slot_of[j] = jnp.minimum(step_of * local + rank, slots - 1)
    else:
        for i in range(slots):
            raw[i, mine] = source[i]
        field_out[...] = field_in[...]
    field[mine] = field_out[...]
    for copy in own[2:]:
        copy.wait()
    pl.semaphore_wait(barrier, greeted)

    def remote(src, dst, send, recv, target):
        return pltpu.make_async_remote_copy(
            src_ref=src, dst_ref=dst, send_sem=send, recv_sem=recv, device_id=target, device_id_type=MESH
        )

    def z_copy(i, step):
        return remote(outgoing.at[i], raw.at[i, mine], z_send.at[i], z_recv.at[i], {"walk": partner(walk, step, walks)})

    def x_copy(i, step):
        return remote(raw.at[i, mine], raw.at[i, mine], x_send.at[step, i], x_recv.at[step, i], {"slab": slab_peer(step)})

    def c_copy(i, hop, step):
        q = slab_source(hop) * cores + core
        return remote(raw.at[i, q], raw.at[i, q], c_send.at[hop, step, i], c_recv.at[hop, step, i], {"row": core_peer(step)})

    def small(src, buf, xs, xr, cs, cr):
        def x(step):
            return remote(src, buf.at[mine], xs.at[step], xr.at[step], {"slab": slab_peer(step)})

        def c(hop, step):
            q = slab_source(hop) * cores + core
            block = src if hop == 0 else buf.at[q]
            return remote(block, buf.at[q], cs.at[hop, step], cr.at[hop, step], {"row": core_peer(step)})

        return x, c

    for i in range(local, slots):
        z_copy(i, i // local).start()
    pairs = [
        small(trial_ref, trial, tx_send, tx_recv, tc_send, tc_recv),
        small(field_out, field, fx_send, fx_recv, fc_send, fc_recv),
    ]
    for x, c in pairs:
        for step in range(1, slabs):
            x(step).start()
        for step in range(1, cores):
            c(0, step).start()
    def spread(i):
        for step in range(1, slabs):
            x_copy(i, step).start()
        for step in range(1, cores):
            c_copy(i, 0, step).start()

    def relay(i):
        for hop in range(1, slabs):
            x_copy(i, hop).wait_recv()
            for step in range(1, cores):
                c_copy(i, hop, step).start()

    def compute(i):
        for hop in range(slabs):
            for step in range(1, cores):
                c_copy(i, hop, step).wait_recv()
        for q in range(slabs * cores):
            column = jnp.transpose(field[q])
            lane = lax.broadcasted_iota(jnp.int32, column.shape, 1)
            scale = jnp.sum(jnp.where(lane == i, column, 0.0), axis=1, keepdims=True)
            prop[q * rows : (q + 1) * rows, :] = (raw[i, q].astype(jnp.float32) * scale).astype(jnp.bfloat16)
        half[i] = dot(chol[...], prop[...]).astype(jnp.bfloat16)

        @pl.when(lax.rem(i, cores) == core)
        def _():
            total = dot(trial[0], prop[0:rows, :])
            for q in range(1, slabs * cores):
                total += dot(trial[q], prop[q * rows : (q + 1) * rows, :])
            inter[i // cores] = total

    for i in range(local):
        spread(i)
    for x, c in pairs:
        for hop in range(1, slabs):
            x(hop).wait_recv()
            for step in range(1, cores):
                c(hop, step).start()
    for x, c in pairs:
        for hop in range(slabs):
            for step in range(1, cores):
                c(hop, step).wait_recv()

    share = slots // cores
    line = lax.broadcasted_iota(jnp.int32, (electrons, electrons), 0)
    diagonal = line == lax.broadcasted_iota(jnp.int32, (electrons, electrons), 1)

    def i_copy(i, step):
        place = inverse.at[i]
        return remote(place, place, i_send.at[i // cores, step], i_recv.at[i // cores, step], {"row": core_peer(step)})

    def first_guess(n):
        matrix = inter[n]
        sizes_of = jnp.abs(matrix)
        column_max = jnp.max(jnp.sum(sizes_of, axis=0, keepdims=True), axis=1, keepdims=True)
        row_max = jnp.max(jnp.sum(sizes_of, axis=1, keepdims=True), axis=0, keepdims=True)
        start = jnp.transpose(matrix) / (column_max * row_max)
        stack[0:electrons, :] = start
        stack[electrons:, :] = dot3(matrix, start)

    def finish(i):
        @pl.when(lax.rem(i, cores) != core)
        def _():
            i_copy(i, lax.rem(core + cores - lax.rem(i, cores), cores)).wait_recv()

        contracted = dot(half[i], inverse[i])
        for g in range(vectors):
            block = contracted[g * electrons : (g + 1) * electrons, :]
            traces[i, g : g + 1, :] = jnp.sum(jnp.where(diagonal, block, 0.0), axis=0, keepdims=True)
            squares[i, g : g + 1, :] = jnp.sum(block * jnp.transpose(block), axis=0, keepdims=True)

    ready = cores + 1

    @pl.loop(0, slots + ready + cores)
    def _(i):
        @pl.when((i >= local) & (i < slots))
        def _():
            z_copy(i, 0).wait_recv()
            spread(i)

        @pl.when((i > 0) & (i <= slots))
        def _():
            relay(i - 1)

        @pl.when((i > 1) & (i < slots + 2))
        def _():
            compute(i - 2)

        for part in range(cores):

            @pl.when((i >= ready) & (i < slots + ready) & (lax.rem(i + cores - 1, cores) == part))
            def _():
                n = (i - ready) // cores
                if part == 0:
                    first_guess(n)

                first, middle, last = ITERS * part // cores, EARLY, ITERS * (part + 1) // cores

                @pl.loop(first, max(first, min(middle, last)))
                def _(iteration):
                    both = stack[...]
                    low = both.astype(jnp.bfloat16)
                    stack[...] = 2.0 * both - dot(low, low[electrons:, :])

                @pl.loop(min(last, max(middle, first)), last)
                def _(iteration):
                    both = stack[...]
                    stack[...] = 2.0 * both - dot3(both, both[electrons:, :])

                if part == cores - 1:
                    inverse[n * cores + core] = stack[0:electrons, :].astype(jnp.bfloat16)
                    for step in range(1, cores):
                        i_copy(n * cores + core, step).start()

        @pl.when(i >= ready + cores)
        def _():
            finish(i - ready - cores)

    alive = lax.broadcasted_iota(jnp.int32, bias_ref.shape, 0) < count_ref[0]
    column = lax.broadcasted_iota(jnp.int32, bias_ref.shape, 1)
    for terms, rows_of, result, factor in ((traces, bias_rows, bias_ref, 1.0), (squares, exch_rows, exch_ref, -0.5)):
        for j in range(slots):
            block = terms[slot_of[j]]
            for g in range(vectors):
                rows_of[g, j : j + 1, :] = block[g : g + 1, :]
        total = jnp.zeros(result.shape, jnp.float32)
        for g in range(vectors):
            total = jnp.where(column == g, jnp.sum(rows_of[g], axis=1, keepdims=True), total)
        result[...] = jnp.where(alive, factor * total, 0.0)

    for i in range(local, slots):
        z_copy(i, i // local).wait_send()

    @pl.loop(0, slots)
    def _(i):
        for step in range(1, slabs):
            x_copy(i, step).wait_send()
        for hop in range(slabs):
            for step in range(1, cores):
                c_copy(i, hop, step).wait_send()

    for x, c in pairs:
        for step in range(1, slabs):
            x(step).wait_send()
        for hop in range(slabs):
            for step in range(1, cores):
                c(hop, step).wait_send()
    for n in range(share):
        for step in range(1, cores):
            i_copy(n * cores + core, step).wait_send()


def on_device(walkers, trial_orbitals, cholesky, branches, counts, field):
    walks, slabs, cores = lax.axis_size("walk"), lax.axis_size("slab"), lax.axis_size("row")
    walk = lax.axis_index("walk")
    per_device, rows, electrons = walkers.shape
    vectors = cholesky.shape[0]
    capacity = (per_device + walks - 1) // walks
    local = capacity if walks * capacity == per_device else per_device
    if local == per_device:
        sender = branches.reshape(walks, per_device) // per_device
        local_index = branches.reshape(walks, per_device) % per_device
        places = jnp.arange(per_device, dtype=jnp.int32)
        same_sender = sender[:, :, None] == sender[:, None, :]
        rank = jnp.sum(same_sender & (places[None, :] < places[:, None])[None], axis=2)
        ranks = jnp.arange(capacity, dtype=jnp.int32)[None, :, None]
        wanted = (sender[:, None, :] == walk) & (rank[:, None, :] == ranks)
        chosen = jnp.sum(jnp.where(wanted, local_index[:, None, :], 0), axis=2)
        outgoing = jnp.take(walkers, chosen.reshape(-1), axis=0, mode="clip")
        outgoing = outgoing.reshape(walks, capacity, rows, electrons)
        arrived = lax.all_to_all(outgoing, "walk", split_axis=0, concat_axis=0, tiled=True)
        arrived = arrived.reshape(walks * capacity, rows, electrons)
        my_sender = lax.dynamic_index_in_dim(sender, walk, 0, keepdims=False)
        my_rank = lax.dynamic_index_in_dim(rank, walk, 0, keepdims=False)
        walkers = jnp.take(arrived, my_sender * capacity + my_rank, axis=0, mode="clip")
    shards = slabs * cores
    share = per_device // cores
    dma = pltpu.SemaphoreType.DMA
    vmem = pl.BlockSpec(memory_space=pltpu.VMEM)
    return pl.pallas_call(
        functools.partial(kernel, (walks, slabs, cores, per_device, local)),
        out_shape=[jax.ShapeDtypeStruct((per_device, vectors), jnp.float32)] * 2,
        in_specs=[pl.BlockSpec(memory_space=pltpu.SMEM)] * 2 + [pl.BlockSpec(memory_space=pl.ANY)] * 4,
        out_specs=[vmem] * 2,
        scratch_shapes=[
            pltpu.VMEM((per_device, rows, electrons), jnp.bfloat16),
            pltpu.VMEM((per_device, rows, electrons), jnp.bfloat16),
            pltpu.VMEM((per_device, rows), jnp.float32),
            pltpu.VMEM((per_device, rows), jnp.float32),
            pltpu.VMEM((per_device, vectors, electrons), jnp.float32),
            pltpu.VMEM((per_device, vectors, electrons), jnp.float32),
            pltpu.VMEM((vectors, per_device, electrons), jnp.float32),
            pltpu.VMEM((vectors, per_device, electrons), jnp.float32),
            pltpu.VMEM((per_device, shards, rows, electrons), jnp.bfloat16),
            pltpu.VMEM((shards, electrons, rows), jnp.bfloat16),
            pltpu.VMEM((shards, per_device, rows), jnp.float32),
            pltpu.VMEM((vectors * electrons, shards * rows), jnp.bfloat16),
            pltpu.VMEM((shards * rows, electrons), jnp.bfloat16),
            pltpu.VMEM((per_device, vectors * electrons, electrons), jnp.bfloat16),
            pltpu.VMEM((share, electrons, electrons), jnp.float32),
            pltpu.VMEM((2 * electrons, electrons), jnp.float32),
            pltpu.VMEM((per_device, electrons, electrons), jnp.bfloat16),
            dma((per_device,)), dma((per_device,)),
            dma((slabs, per_device)), dma((slabs, per_device)),
            dma((slabs, cores, per_device)), dma((slabs, cores, per_device)),
            dma((share, cores)), dma((share, cores)),
            dma((slabs,)), dma((slabs,)), dma((slabs, cores)), dma((slabs, cores)),
            dma((slabs,)), dma((slabs,)), dma((slabs, cores)), dma((slabs, cores)),
            dma((4,)),
        ],
        compiler_params=pltpu.CompilerParams(
            collective_id=0, has_side_effects=True, vmem_limit_bytes=48 * 1024 * 1024
        ),
    )(branches, counts, walkers, trial_orbitals.T, cholesky.reshape(vectors * electrons, shards * rows), field)


def solution(mesh):
    return jax.shard_map(
        on_device,
        mesh=mesh,
        in_specs=(
            P(("parts", "walk"), ("slab", "row"), None),
            P(("parts", "slab", "row"), None),
            P(("parts", "slab", "row"), None, None),
            P("parts"),
            P(("parts", "walk")),
            P(("parts", "walk"), ("slab", "row")),
        ),
        out_specs=(P(("parts", "walk"), ("slab", "row")), P(("parts", "walk"), ("slab", "row"))),
        check_vma=False,
    )
```

```python
import functools

import jax
import jax.numpy as jnp
from jax import lax
from jax.experimental import pallas as pl
from jax.experimental.pallas import tpu as pltpu
from jax.sharding import PartitionSpec as P

ITERS = 10
EARLY = 4
MESH = pl.DeviceIdType.MESH


def split(x):
    high = x.astype(jnp.bfloat16)
    low = (x - high.astype(jnp.float32)).astype(jnp.bfloat16)
    return high, low


def dot(a, b):
    return jnp.dot(a, b, preferred_element_type=jnp.float32)


def dot3(a, b):
    ah, al = split(a)
    bh, bl = split(b)
    return dot(ah, bh) + (dot(ah, bl) + dot(al, bh))


def partner(position, step, size):
    if size & (size - 1):
        return (position + step) % size
    result, bit = 0, 1
    while bit < size:
        digit = (position // bit) % 2
        result += bit * (1 - digit if step & bit else digit)
        bit *= 2
    return result


def kernel(
    sizes, branch_in, walker_ref, trial_ref, chol_ref, field_ref, bias_ref, exch_ref,
    branch_ref, trial_t, source, outgoing, field_in, field_out, traces, squares, bias_rows, exch_rows, raw, trial, field, chol, prop, half, inter, stack, inverse,
    z_send, z_recv, x_send, x_recv, c_send, c_recv, i_send, i_recv,
    tx_send, tx_recv, tc_send, tc_recv, fx_send, fx_recv, fc_send, fc_recv, own_sem,
):
    walks, slabs, cores, slots, local = sizes
    walk, slab, core = lax.axis_index("walk"), lax.axis_index("slab"), lax.axis_index("row")
    rows, electrons = trial_ref.shape
    vectors = chol_ref.shape[0] // electrons
    mine = slab * cores + core

    def slab_peer(step):
        return lax.rem(slab + step, slabs)

    def core_peer(step):
        return lax.rem(core + step, cores)

    def slab_source(step):
        return lax.rem(slab + slabs - step, slabs)

    def core_source(step):
        return lax.rem(core + cores - step, cores)

    loads = [(branch_in, branch_ref), (walker_ref, source), (field_ref, field_in), (trial_ref, trial.at[mine]), (chol_ref, chol)]
    own = [pltpu.make_async_copy(src, dst, own_sem.at[k]) for k, (src, dst) in enumerate(loads)]
    for copy in own:
        copy.start()
    barrier = pltpu.get_barrier_semaphore()
    greeted = 0
    if local < slots:
        for step in range(1, walks):
            pl.semaphore_signal(barrier, inc=1, device_id={"walk": partner(walk, step, walks)}, device_id_type=MESH)
            greeted += 1
    for step in range(1, slabs):
        pl.semaphore_signal(barrier, inc=1, device_id={"slab": slab_peer(step)}, device_id_type=MESH)
        greeted += 1
    for step in range(1, cores):
        pl.semaphore_signal(barrier, inc=1, device_id={"row": core_peer(step)}, device_id_type=MESH)
        greeted += 1

    def sender(w, k):
        return lax.div(branch_ref[w * slots + k], slots)

    def kth(w, origin, values):
        picks, count = [jnp.int32(0)] * local, jnp.int32(0)
        for k in range(slots):
            hit = sender(w, k) == origin
            picks = [jnp.where(hit & (count == place), values(k), pick) for place, pick in enumerate(picks)]
            count = count + jnp.where(hit, 1, 0)
        return picks

    for copy in own[:3]:
        copy.wait()
    slot_of = list(range(slots))
    if local < slots:
        origins = []
        for step in range(walks):
            target = partner(walk, step, walks)
            picks = kth(target, walk, lambda k: lax.rem(branch_ref[target * slots + k], slots))
            for place, pick in enumerate(picks):
                if step == 0:
                    raw[place, mine] = source[pick]
                else:
                    outgoing[step * local + place] = source[pick]
            origin = target if walks & (walks - 1) == 0 else (walk + walks - step) % walks
            origins.append(origin)
            for place, pick in enumerate(kth(walk, origin, lambda k: k)):
                i = step * local + place
                field_out[i : i + 1, :] = field_in[pl.ds(pick, 1), :]
        for j in range(slots):
            origin, rank, step_of = sender(walk, j), jnp.int32(0), jnp.int32(0)
            for k in range(j):
                rank = rank + jnp.where(sender(walk, k) == origin, 1, 0)
            for step in range(walks):
                step_of = jnp.where(origins[step] == origin, step, step_of)
            slot_of[j] = jnp.minimum(step_of * local + rank, slots - 1)
    else:
        for i in range(slots):
            raw[i, mine] = source[i]
        field_out[...] = field_in[...]
    field[mine] = field_out[...]
    for copy in own[3:]:
        copy.wait()
    pl.semaphore_wait(barrier, greeted)

    def remote(src, dst, send, recv, target):
        return pltpu.make_async_remote_copy(
            src_ref=src, dst_ref=dst, send_sem=send, recv_sem=recv, device_id=target, device_id_type=MESH
        )

    def z_copy(i, step):
        return remote(outgoing.at[i], raw.at[i, mine], z_send.at[i], z_recv.at[i], {"walk": partner(walk, step, walks)})

    def x_copy(i, step):
        return remote(raw.at[i, mine], raw.at[i, mine], x_send.at[step, i], x_recv.at[step, i], {"slab": slab_peer(step)})

    def c_copy(i, hop, step):
        q = slab_source(hop) * cores + core
        return remote(raw.at[i, q], raw.at[i, q], c_send.at[hop, step, i], c_recv.at[hop, step, i], {"row": core_peer(step)})

    def small(src, buf, xs, xr, cs, cr):
        def x(step):
            return remote(src, buf.at[mine], xs.at[step], xr.at[step], {"slab": slab_peer(step)})

        def c(hop, step):
            q = slab_source(hop) * cores + core
            block = src if hop == 0 else buf.at[q]
            return remote(block, buf.at[q], cs.at[hop, step], cr.at[hop, step], {"row": core_peer(step)})

        return x, c

    for i in range(local, slots):
        z_copy(i, i // local).start()
    pairs = [
        small(trial_ref, trial, tx_send, tx_recv, tc_send, tc_recv),
        small(field_out, field, fx_send, fx_recv, fc_send, fc_recv),
    ]
    for x, c in pairs:
        for step in range(1, slabs):
            x(step).start()
        for step in range(1, cores):
            c(0, step).start()
    def spread(i):
        for step in range(1, slabs):
            x_copy(i, step).start()
        for step in range(1, cores):
            c_copy(i, 0, step).start()

    def relay(i):
        for hop in range(1, slabs):
            x_copy(i, hop).wait_recv()
            for step in range(1, cores):
                c_copy(i, hop, step).start()

    def compute(i):
        for hop in range(slabs):
            for step in range(1, cores):
                c_copy(i, hop, step).wait_recv()
        for q in range(slabs * cores):
            column = jnp.transpose(field[q])
            lane = lax.broadcasted_iota(jnp.int32, column.shape, 1)
            scale = jnp.sum(jnp.where(lane == i, column, 0.0), axis=1, keepdims=True)
            prop[q * rows : (q + 1) * rows, :] = (raw[i, q].astype(jnp.float32) * scale).astype(jnp.bfloat16)
        @pl.when(lax.rem(i, cores) == core)
        def _():
            total = dot(trial_t[0], prop[0:rows, :])
            for q in range(1, slabs * cores):
                total += dot(trial_t[q], prop[q * rows : (q + 1) * rows, :])
            inter[i // cores] = total

        half[i] = dot(chol[...], prop[...]).astype(jnp.bfloat16)

    for i in range(local):
        spread(i)
    for x, c in pairs:
        for hop in range(1, slabs):
            x(hop).wait_recv()
            for step in range(1, cores):
                c(hop, step).start()
    for x, c in pairs:
        for hop in range(slabs):
            for step in range(1, cores):
                c(hop, step).wait_recv()

    for q in range(slabs * cores):
        trial_t[q] = jnp.transpose(trial[q].astype(jnp.float32)).astype(jnp.bfloat16)
    share = slots // cores
    line = lax.broadcasted_iota(jnp.int32, (electrons, electrons), 0)
    diagonal = line == lax.broadcasted_iota(jnp.int32, (electrons, electrons), 1)

    def i_copy(i, step):
        place = inverse.at[i]
        return remote(place, place, i_send.at[i // cores, step], i_recv.at[i // cores, step], {"row": core_peer(step)})

    def first_guess(n):
        matrix = inter[n]
        sizes_of = jnp.abs(matrix)
        column_max = jnp.max(jnp.sum(sizes_of, axis=0, keepdims=True), axis=1, keepdims=True)
        row_max = jnp.max(jnp.sum(sizes_of, axis=1, keepdims=True), axis=0, keepdims=True)
        start = jnp.transpose(matrix) / (column_max * row_max)
        stack[0:electrons, :] = start
        stack[electrons:, :] = dot3(matrix, start)

    def finish(i):
        @pl.when(lax.rem(i, cores) != core)
        def _():
            i_copy(i, lax.rem(core + cores - lax.rem(i, cores), cores)).wait_recv()

        contracted = dot(half[i], inverse[i])
        for g in range(vectors):
            block = contracted[g * electrons : (g + 1) * electrons, :]
            traces[i, g : g + 1, :] = jnp.sum(jnp.where(diagonal, block, 0.0), axis=0, keepdims=True)
            squares[i, g : g + 1, :] = jnp.sum(block * jnp.transpose(block), axis=0, keepdims=True)

    ready = cores + 1

    @pl.loop(0, slots + ready + cores + 1)
    def _(i):
        @pl.when((i >= local) & (i < slots))
        def _():
            z_copy(i, 0).wait_recv()
            spread(i)

        @pl.when((i > 1) & (i < slots + 2))
        def _():
            compute(i - 2)

        for part in range(cores):

            @pl.when((i >= ready) & (i < slots + ready) & (lax.rem(i + cores - 1, cores) == part))
            def _():
                n = (i - ready) // cores
                if part == 0:
                    first_guess(n)

                first, middle, last = ITERS * part // cores, EARLY, ITERS * (part + 1) // cores

                @pl.loop(first, max(first, min(middle, last)))
                def _(iteration):
                    both = stack[...]
                    low = both.astype(jnp.bfloat16)
                    stack[...] = 2.0 * both - dot(low, low[electrons:, :])

                @pl.loop(min(last, max(middle, first)), last)
                def _(iteration):
                    both = stack[...]
                    stack[...] = 2.0 * both - dot3(both, both[electrons:, :])

                if part == cores - 1:
                    inverse[n * cores + core] = stack[0:electrons, :].astype(jnp.bfloat16)
                    for step in range(1, cores):
                        i_copy(n * cores + core, step).start()

        @pl.when(i > ready + cores)
        def _():
            finish(i - ready - cores - 1)

        @pl.when((i > 0) & (i <= slots))
        def _():
            relay(i - 1)

    column = lax.broadcasted_iota(jnp.int32, bias_ref.shape, 1)
    for terms, rows_of, result in ((traces, bias_rows, bias_ref), (squares, exch_rows, exch_ref)):
        for j in range(slots):
            block = terms[slot_of[j]]
            for g in range(vectors):
                rows_of[g, j : j + 1, :] = block[g : g + 1, :]
        total = jnp.zeros(result.shape, jnp.float32)
        for g in range(vectors):
            total = jnp.where(column == g, jnp.sum(rows_of[g], axis=1, keepdims=True), total)
        result[...] = total

    for i in range(local, slots):
        z_copy(i, i // local).wait_send()

    @pl.loop(0, slots)
    def _(i):
        for step in range(1, slabs):
            x_copy(i, step).wait_send()
        for hop in range(slabs):
            for step in range(1, cores):
                c_copy(i, hop, step).wait_send()

    for x, c in pairs:
        for step in range(1, slabs):
            x(step).wait_send()
        for hop in range(slabs):
            for step in range(1, cores):
                c(hop, step).wait_send()
    for n in range(share):
        for step in range(1, cores):
            i_copy(n * cores + core, step).wait_send()


def on_device(walkers, trial_orbitals, cholesky, branches, counts, field):
    walks, slabs, cores = lax.axis_size("walk"), lax.axis_size("slab"), lax.axis_size("row")
    walk = lax.axis_index("walk")
    per_device, rows, electrons = walkers.shape
    vectors = cholesky.shape[0]
    capacity = (per_device + walks - 1) // walks
    local = capacity if walks * capacity == per_device else per_device
    if local == per_device:
        sender = branches.reshape(walks, per_device) // per_device
        local_index = branches.reshape(walks, per_device) % per_device
        places = jnp.arange(per_device, dtype=jnp.int32)
        same_sender = sender[:, :, None] == sender[:, None, :]
        rank = jnp.sum(same_sender & (places[None, :] < places[:, None])[None], axis=2)
        ranks = jnp.arange(capacity, dtype=jnp.int32)[None, :, None]
        wanted = (sender[:, None, :] == walk) & (rank[:, None, :] == ranks)
        chosen = jnp.sum(jnp.where(wanted, local_index[:, None, :], 0), axis=2)
        outgoing = jnp.take(walkers, chosen.reshape(-1), axis=0, mode="clip")
        outgoing = outgoing.reshape(walks, capacity, rows, electrons)
        arrived = lax.all_to_all(outgoing, "walk", split_axis=0, concat_axis=0, tiled=True)
        arrived = arrived.reshape(walks * capacity, rows, electrons)
        my_sender = lax.dynamic_index_in_dim(sender, walk, 0, keepdims=False)
        my_rank = lax.dynamic_index_in_dim(rank, walk, 0, keepdims=False)
        walkers = jnp.take(arrived, my_sender * capacity + my_rank, axis=0, mode="clip")
    shards = slabs * cores
    share = per_device // cores
    dma = pltpu.SemaphoreType.DMA
    vmem = pl.BlockSpec(memory_space=pltpu.VMEM)
    bias, exchange = pl.pallas_call(
        functools.partial(kernel, (walks, slabs, cores, per_device, local)),
        out_shape=[jax.ShapeDtypeStruct((per_device, vectors), jnp.float32)] * 2,
        in_specs=[pl.BlockSpec(memory_space=pl.ANY)] * 5,
        out_specs=[vmem] * 2,
        scratch_shapes=[
            pltpu.SMEM(branches.shape, jnp.int32),
            pltpu.VMEM((shards, electrons, rows), jnp.bfloat16),
            pltpu.VMEM((per_device, rows, electrons), jnp.bfloat16),
            pltpu.VMEM((per_device, rows, electrons), jnp.bfloat16),
            pltpu.VMEM((per_device, rows), jnp.float32),
            pltpu.VMEM((per_device, rows), jnp.float32),
            pltpu.VMEM((per_device, vectors, electrons), jnp.float32),
            pltpu.VMEM((per_device, vectors, electrons), jnp.float32),
            pltpu.VMEM((vectors, per_device, electrons), jnp.float32),
            pltpu.VMEM((vectors, per_device, electrons), jnp.float32),
            pltpu.VMEM((per_device, shards, rows, electrons), jnp.bfloat16),
            pltpu.VMEM((shards, rows, electrons), jnp.bfloat16),
            pltpu.VMEM((shards, per_device, rows), jnp.float32),
            pltpu.VMEM((vectors * electrons, shards * rows), jnp.bfloat16),
            pltpu.VMEM((shards * rows, electrons), jnp.bfloat16),
            pltpu.VMEM((per_device, vectors * electrons, electrons), jnp.bfloat16),
            pltpu.VMEM((share, electrons, electrons), jnp.float32),
            pltpu.VMEM((2 * electrons, electrons), jnp.float32),
            pltpu.VMEM((per_device, electrons, electrons), jnp.bfloat16),
            dma((per_device,)), dma((per_device,)),
            dma((slabs, per_device)), dma((slabs, per_device)),
            dma((slabs, cores, per_device)), dma((slabs, cores, per_device)),
            dma((share, cores)), dma((share, cores)),
            dma((slabs,)), dma((slabs,)), dma((slabs, cores)), dma((slabs, cores)),
            dma((slabs,)), dma((slabs,)), dma((slabs, cores)), dma((slabs, cores)),
            dma((5,)),
        ],
        compiler_params=pltpu.CompilerParams(
            collective_id=0, has_side_effects=True, vmem_limit_bytes=48 * 1024 * 1024
        ),
    )(branches, walkers, trial_orbitals, cholesky.reshape(vectors * electrons, shards * rows), field)
    living = (jnp.arange(per_device, dtype=jnp.int32) < counts[0]).astype(jnp.float32)[:, None]
    return bias * living, -0.5 * exchange * living


def solution(mesh):
    return jax.shard_map(
        on_device,
        mesh=mesh,
        in_specs=(
            P(("parts", "walk"), ("slab", "row"), None),
            P(("parts", "slab", "row"), None),
            P(("parts", "slab", "row"), None, None),
            P("parts"),
            P(("parts", "walk")),
            P(("parts", "walk"), ("slab", "row")),
        ),
        out_specs=(P(("parts", "walk"), ("slab", "row")), P(("parts", "walk"), ("slab", "row"))),
        check_vma=False,
    )
```

```python
import functools

import jax
import jax.numpy as jnp
from jax import lax
from jax.experimental import pallas as pl
from jax.experimental.pallas import tpu as pltpu
from jax.sharding import PartitionSpec as P

ITERS = 10
EARLY = 4
MESH = pl.DeviceIdType.MESH


def split(x):
    high = x.astype(jnp.bfloat16)
    low = (x - high.astype(jnp.float32)).astype(jnp.bfloat16)
    return high, low


def dot(a, b):
    return jnp.dot(a, b, preferred_element_type=jnp.float32)


def dot3(a, b):
    ah, al = split(a)
    bh, bl = split(b)
    return dot(ah, bh) + (dot(ah, bl) + dot(al, bh))


def partner(position, step, size):
    if size & (size - 1):
        return (position + step) % size
    result, bit = 0, 1
    while bit < size:
        digit = (position // bit) % 2
        result += bit * (1 - digit if step & bit else digit)
        bit *= 2
    return result


def kernel(
    sizes, branch_in, walker_ref, trial_ref, chol_ref, field_ref, bias_ref, exch_ref,
    branch_ref, trial_t, source, outgoing, field_in, field_out, traces, squares, bias_rows, exch_rows, raw, trial, field, chol, prop, half, inter, stack, inverse,
    z_send, z_recv, x_send, x_recv, c_send, c_recv, i_send, i_recv,
    tx_send, tx_recv, tc_send, tc_recv, fx_send, fx_recv, fc_send, fc_recv, own_sem,
):
    walks, slabs, cores, slots, local = sizes
    walk, slab, core = lax.axis_index("walk"), lax.axis_index("slab"), lax.axis_index("row")
    rows, electrons = trial_ref.shape
    vectors = chol_ref.shape[0] // electrons
    mine = slab * cores + core

    def slab_peer(step):
        return lax.rem(slab + step, slabs)

    def core_peer(step):
        return lax.rem(core + step, cores)

    def slab_source(step):
        return lax.rem(slab + slabs - step, slabs)

    def core_source(step):
        return lax.rem(core + cores - step, cores)

    loads = [(branch_in, branch_ref), (walker_ref, source), (field_ref, field_in), (trial_ref, trial.at[mine]), (chol_ref, chol)]
    own = [pltpu.make_async_copy(src, dst, own_sem.at[k]) for k, (src, dst) in enumerate(loads)]
    for copy in own:
        copy.start()
    barrier = pltpu.get_barrier_semaphore()
    greeted = 0
    if local < slots:
        for step in range(1, walks):
            pl.semaphore_signal(barrier, inc=1, device_id={"walk": partner(walk, step, walks)}, device_id_type=MESH)
            greeted += 1
    for step in range(1, slabs):
        pl.semaphore_signal(barrier, inc=1, device_id={"slab": slab_peer(step)}, device_id_type=MESH)
        greeted += 1
    for step in range(1, cores):
        pl.semaphore_signal(barrier, inc=1, device_id={"row": core_peer(step)}, device_id_type=MESH)
        greeted += 1

    def sender(w, k):
        return lax.div(branch_ref[w * slots + k], slots)

    def kth(w, origin, values):
        picks, count = [jnp.int32(0)] * local, jnp.int32(0)
        for k in range(slots):
            hit = sender(w, k) == origin
            picks = [jnp.where(hit & (count == place), values(k), pick) for place, pick in enumerate(picks)]
            count = count + jnp.where(hit, 1, 0)
        return picks

    for copy in own[:3]:
        copy.wait()
    slot_of = list(range(slots))
    if local < slots:
        origins = []
        for step in range(walks):
            target = partner(walk, step, walks)
            picks = kth(target, walk, lambda k: lax.rem(branch_ref[target * slots + k], slots))
            for place, pick in enumerate(picks):
                if step == 0:
                    raw[place, mine] = source[pick]
                else:
                    outgoing[step * local + place] = source[pick]
            origin = target if walks & (walks - 1) == 0 else (walk + walks - step) % walks
            origins.append(origin)
            for place, pick in enumerate(kth(walk, origin, lambda k: k)):
                i = step * local + place
                field_out[i : i + 1, :] = field_in[pl.ds(pick, 1), :]
        for j in range(slots):
            origin, rank, step_of = sender(walk, j), jnp.int32(0), jnp.int32(0)
            for k in range(j):
                rank = rank + jnp.where(sender(walk, k) == origin, 1, 0)
            for step in range(walks):
                step_of = jnp.where(origins[step] == origin, step, step_of)
            slot_of[j] = jnp.minimum(step_of * local + rank, slots - 1)
    else:
        for i in range(slots):
            raw[i, mine] = source[i]
        field_out[...] = field_in[...]
    field[mine] = field_out[...]
    for copy in own[3:]:
        copy.wait()
    pl.semaphore_wait(barrier, greeted)

    def remote(src, dst, send, recv, target):
        return pltpu.make_async_remote_copy(
            src_ref=src, dst_ref=dst, send_sem=send, recv_sem=recv, device_id=target, device_id_type=MESH
        )

    def z_copy(i, step):
        return remote(outgoing.at[i], raw.at[i, mine], z_send.at[i], z_recv.at[i], {"walk": partner(walk, step, walks)})

    def x_copy(i, step):
        return remote(raw.at[i, mine], raw.at[i, mine], x_send.at[step, i], x_recv.at[step, i], {"slab": slab_peer(step)})

    def c_copy(i, hop, step):
        q = slab_source(hop) * cores + core
        return remote(raw.at[i, q], raw.at[i, q], c_send.at[hop, step, i], c_recv.at[hop, step, i], {"row": core_peer(step)})

    def small(src, buf, xs, xr, cs, cr):
        def x(step):
            return remote(src, buf.at[mine], xs.at[step], xr.at[step], {"slab": slab_peer(step)})

        def c(hop, step):
            q = slab_source(hop) * cores + core
            block = src if hop == 0 else buf.at[q]
            return remote(block, buf.at[q], cs.at[hop, step], cr.at[hop, step], {"row": core_peer(step)})

        return x, c

    for i in range(local, slots):
        z_copy(i, i // local).start()
    pairs = [
        small(trial_ref, trial, tx_send, tx_recv, tc_send, tc_recv),
        small(field_out, field, fx_send, fx_recv, fc_send, fc_recv),
    ]
    for x, c in pairs:
        for step in range(1, slabs):
            x(step).start()
        for step in range(1, cores):
            c(0, step).start()
    def spread(i):
        for step in range(1, slabs):
            x_copy(i, step).start()
        for step in range(1, cores):
            c_copy(i, 0, step).start()

    def relay(i):
        for hop in range(1, slabs):
            x_copy(i, hop).wait_recv()
            for step in range(1, cores):
                c_copy(i, hop, step).start()

    def compute(i):
        for hop in range(slabs):
            for step in range(1, cores):
                c_copy(i, hop, step).wait_recv()
        for q in range(slabs * cores):
            column = jnp.transpose(field[q])
            lane = lax.broadcasted_iota(jnp.int32, column.shape, 1)
            scale = jnp.sum(jnp.where(lane == i, column, 0.0), axis=1, keepdims=True)
            prop[q * rows : (q + 1) * rows, :] = (raw[i, q].astype(jnp.float32) * scale).astype(jnp.bfloat16)
        @pl.when(lax.rem(i, cores) == core)
        def _():
            total = dot(trial_t[0], prop[0:rows, :])
            for q in range(1, slabs * cores):
                total += dot(trial_t[q], prop[q * rows : (q + 1) * rows, :])
            inter[i // cores] = total

        half[i] = dot(chol[...], prop[...]).astype(jnp.bfloat16)

    for i in range(local):
        spread(i)
    for x, c in pairs:
        for hop in range(1, slabs):
            x(hop).wait_recv()
            for step in range(1, cores):
                c(hop, step).start()
    for x, c in pairs:
        for hop in range(slabs):
            for step in range(1, cores):
                c(hop, step).wait_recv()

    for q in range(slabs * cores):
        trial_t[q] = jnp.transpose(trial[q].astype(jnp.float32)).astype(jnp.bfloat16)
    share = slots // cores
    line = lax.broadcasted_iota(jnp.int32, (electrons, electrons), 0)
    diagonal = line == lax.broadcasted_iota(jnp.int32, (electrons, electrons), 1)

    def i_copy(i, step):
        place = inverse.at[i]
        return remote(place, place, i_send.at[i // cores, step], i_recv.at[i // cores, step], {"row": core_peer(step)})

    def first_guess(n):
        matrix = inter[n]
        sizes_of = jnp.abs(matrix)
        column_max = jnp.max(jnp.sum(sizes_of, axis=0, keepdims=True), axis=1, keepdims=True)
        row_max = jnp.max(jnp.sum(sizes_of, axis=1, keepdims=True), axis=0, keepdims=True)
        start = jnp.transpose(matrix) / (column_max * row_max)
        stack[0:electrons, :] = start
        stack[electrons:, :] = dot3(matrix, start)

    def finish(i):
        @pl.when(lax.rem(i, cores) != core)
        def _():
            i_copy(i, lax.rem(core + cores - lax.rem(i, cores), cores)).wait_recv()

        contracted = dot(half[i], inverse[i])
        for g in range(vectors):
            block = contracted[g * electrons : (g + 1) * electrons, :]
            traces[i, g : g + 1, :] = jnp.sum(jnp.where(diagonal, block, 0.0), axis=0, keepdims=True)
            squares[i, g : g + 1, :] = jnp.sum(block * jnp.transpose(block), axis=0, keepdims=True)

    ready = cores + 1

    @pl.loop(0, slots + ready + cores + 1)
    def _(i):
        @pl.when((i >= local) & (i < slots))
        def _():
            z_copy(i, 0).wait_recv()
            spread(i)

        @pl.when((i > 1) & (i < slots + 2))
        def _():
            compute(i - 2)

        @pl.when((i > 0) & (i <= slots))
        def _():
            relay(i - 1)

        for part in range(cores):

            @pl.when((i >= ready) & (i < slots + ready) & (lax.rem(i + cores - 1, cores) == part))
            def _():
                n = (i - ready) // cores
                if part == 0:
                    first_guess(n)

                first, middle, last = ITERS * part // cores, EARLY, ITERS * (part + 1) // cores

                @pl.loop(first, max(first, min(middle, last)))
                def _(iteration):
                    both = stack[...]
                    low = both.astype(jnp.bfloat16)
                    stack[...] = 2.0 * both - dot(low, low[electrons:, :])

                @pl.loop(min(last, max(middle, first)), last)
                def _(iteration):
                    both = stack[...]
                    stack[...] = 2.0 * both - dot3(both, both[electrons:, :])

                if part == cores - 1:
                    inverse[n * cores + core] = stack[0:electrons, :].astype(jnp.bfloat16)
                    for step in range(1, cores):
                        i_copy(n * cores + core, step).start()

        @pl.when(i > ready + cores)
        def _():
            finish(i - ready - cores - 1)


    column = lax.broadcasted_iota(jnp.int32, bias_ref.shape, 1)
    for terms, rows_of, result in ((traces, bias_rows, bias_ref), (squares, exch_rows, exch_ref)):
        for j in range(slots):
            block = terms[slot_of[j]]
            for g in range(vectors):
                rows_of[g, j : j + 1, :] = block[g : g + 1, :]
        total = jnp.zeros(result.shape, jnp.float32)
        for g in range(vectors):
            total = jnp.where(column == g, jnp.sum(rows_of[g], axis=1, keepdims=True), total)
        result[...] = total

    for i in range(local, slots):
        z_copy(i, i // local).wait_send()

    @pl.loop(0, slots)
    def _(i):
        for step in range(1, slabs):
            x_copy(i, step).wait_send()
        for hop in range(slabs):
            for step in range(1, cores):
                c_copy(i, hop, step).wait_send()

    for x, c in pairs:
        for step in range(1, slabs):
            x(step).wait_send()
        for hop in range(slabs):
            for step in range(1, cores):
                c(hop, step).wait_send()
    for n in range(share):
        for step in range(1, cores):
            i_copy(n * cores + core, step).wait_send()


def on_device(walkers, trial_orbitals, cholesky, branches, counts, field):
    walks, slabs, cores = lax.axis_size("walk"), lax.axis_size("slab"), lax.axis_size("row")
    walk = lax.axis_index("walk")
    per_device, rows, electrons = walkers.shape
    vectors = cholesky.shape[0]
    capacity = (per_device + walks - 1) // walks
    local = capacity if walks * capacity == per_device else per_device
    if local == per_device:
        sender = branches.reshape(walks, per_device) // per_device
        local_index = branches.reshape(walks, per_device) % per_device
        places = jnp.arange(per_device, dtype=jnp.int32)
        same_sender = sender[:, :, None] == sender[:, None, :]
        rank = jnp.sum(same_sender & (places[None, :] < places[:, None])[None], axis=2)
        ranks = jnp.arange(capacity, dtype=jnp.int32)[None, :, None]
        wanted = (sender[:, None, :] == walk) & (rank[:, None, :] == ranks)
        chosen = jnp.sum(jnp.where(wanted, local_index[:, None, :], 0), axis=2)
        outgoing = jnp.take(walkers, chosen.reshape(-1), axis=0, mode="clip")
        outgoing = outgoing.reshape(walks, capacity, rows, electrons)
        arrived = lax.all_to_all(outgoing, "walk", split_axis=0, concat_axis=0, tiled=True)
        arrived = arrived.reshape(walks * capacity, rows, electrons)
        my_sender = lax.dynamic_index_in_dim(sender, walk, 0, keepdims=False)
        my_rank = lax.dynamic_index_in_dim(rank, walk, 0, keepdims=False)
        walkers = jnp.take(arrived, my_sender * capacity + my_rank, axis=0, mode="clip")
    shards = slabs * cores
    share = per_device // cores
    dma = pltpu.SemaphoreType.DMA
    vmem = pl.BlockSpec(memory_space=pltpu.VMEM)
    bias, exchange = pl.pallas_call(
        functools.partial(kernel, (walks, slabs, cores, per_device, local)),
        out_shape=[jax.ShapeDtypeStruct((per_device, vectors), jnp.float32)] * 2,
        in_specs=[pl.BlockSpec(memory_space=pl.ANY)] * 5,
        out_specs=[vmem] * 2,
        scratch_shapes=[
            pltpu.SMEM(branches.shape, jnp.int32),
            pltpu.VMEM((shards, electrons, rows), jnp.bfloat16),
            pltpu.VMEM((per_device, rows, electrons), jnp.bfloat16),
            pltpu.VMEM((per_device, rows, electrons), jnp.bfloat16),
            pltpu.VMEM((per_device, rows), jnp.float32),
            pltpu.VMEM((per_device, rows), jnp.float32),
            pltpu.VMEM((per_device, vectors, electrons), jnp.float32),
            pltpu.VMEM((per_device, vectors, electrons), jnp.float32),
            pltpu.VMEM((vectors, per_device, electrons), jnp.float32),
            pltpu.VMEM((vectors, per_device, electrons), jnp.float32),
            pltpu.VMEM((per_device, shards, rows, electrons), jnp.bfloat16),
            pltpu.VMEM((shards, rows, electrons), jnp.bfloat16),
            pltpu.VMEM((shards, per_device, rows), jnp.float32),
            pltpu.VMEM((vectors * electrons, shards * rows), jnp.bfloat16),
            pltpu.VMEM((shards * rows, electrons), jnp.bfloat16),
            pltpu.VMEM((per_device, vectors * electrons, electrons), jnp.bfloat16),
            pltpu.VMEM((share, electrons, electrons), jnp.float32),
            pltpu.VMEM((2 * electrons, electrons), jnp.float32),
            pltpu.VMEM((per_device, electrons, electrons), jnp.bfloat16),
            dma((per_device,)), dma((per_device,)),
            dma((slabs, per_device)), dma((slabs, per_device)),
            dma((slabs, cores, per_device)), dma((slabs, cores, per_device)),
            dma((share, cores)), dma((share, cores)),
            dma((slabs,)), dma((slabs,)), dma((slabs, cores)), dma((slabs, cores)),
            dma((slabs,)), dma((slabs,)), dma((slabs, cores)), dma((slabs, cores)),
            dma((5,)),
        ],
        compiler_params=pltpu.CompilerParams(
            collective_id=0, has_side_effects=True, vmem_limit_bytes=63 * 1024 * 1024
        ),
    )(branches, walkers, trial_orbitals, cholesky.reshape(vectors * electrons, shards * rows), field)
    living = (jnp.arange(per_device, dtype=jnp.int32) < counts[0]).astype(jnp.float32)[:, None]
    return bias * living, -0.5 * exchange * living


def solution(mesh):
    return jax.shard_map(
        on_device,
        mesh=mesh,
        in_specs=(
            P(("parts", "walk"), ("slab", "row"), None),
            P(("parts", "slab", "row"), None),
            P(("parts", "slab", "row"), None, None),
            P("parts"),
            P(("parts", "walk")),
            P(("parts", "walk"), ("slab", "row")),
        ),
        out_specs=(P(("parts", "walk"), ("slab", "row")), P(("parts", "walk"), ("slab", "row"))),
        check_vma=False,
    )
```

```python
import functools

import jax
import jax.numpy as jnp
from jax import lax
from jax.experimental import pallas as pl
from jax.experimental.pallas import tpu as pltpu
from jax.sharding import PartitionSpec as P

ITERS = 10
EARLY = 4
MESH = pl.DeviceIdType.MESH


def split(x):
    high = x.astype(jnp.bfloat16)
    low = (x - high.astype(jnp.float32)).astype(jnp.bfloat16)
    return high, low


def dot(a, b):
    return jnp.dot(a, b, preferred_element_type=jnp.float32)


def dot3(a, b):
    ah, al = split(a)
    bh, bl = split(b)
    return dot(ah, bh) + (dot(ah, bl) + dot(al, bh))


def partner(position, step, size):
    if size & (size - 1):
        return (position + step) % size
    result, bit = 0, 1
    while bit < size:
        digit = (position // bit) % 2
        result += bit * (1 - digit if step & bit else digit)
        bit *= 2
    return result


def kernel(
    sizes, branch_in, walker_ref, trial_ref, chol_ref, field_ref, bias_ref, exch_ref,
    branch_ref, trial_t, source, outgoing, field_in, field_out, traces, squares, bias_rows, exch_rows, raw, trial, field, chol, prop, half, inter, stack, inverse,
    z_send, z_recv, x_send, x_recv, c_send, c_recv, i_send, i_recv,
    tx_send, tx_recv, tc_send, tc_recv, fx_send, fx_recv, fc_send, fc_recv, own_sem,
):
    walks, slabs, cores, slots, local = sizes
    walk, slab, core = lax.axis_index("walk"), lax.axis_index("slab"), lax.axis_index("row")
    rows, electrons = trial_ref.shape
    vectors = chol_ref.shape[0] // electrons
    mine = slab * cores + core

    def slab_peer(step):
        return lax.rem(slab + step, slabs)

    def core_peer(step):
        return lax.rem(core + step, cores)

    def slab_source(step):
        return lax.rem(slab + slabs - step, slabs)

    def core_source(step):
        return lax.rem(core + cores - step, cores)

    loads = [(branch_in, branch_ref), (walker_ref, source), (field_ref, field_in), (trial_ref, trial.at[mine]), (chol_ref, chol)]
    own = [pltpu.make_async_copy(src, dst, own_sem.at[k]) for k, (src, dst) in enumerate(loads)]
    for copy in own:
        copy.start()
    barrier = pltpu.get_barrier_semaphore()
    greeted = 0
    if local < slots:
        for step in range(1, walks):
            pl.semaphore_signal(barrier, inc=1, device_id={"walk": partner(walk, step, walks)}, device_id_type=MESH)
            greeted += 1
    for step in range(1, slabs):
        pl.semaphore_signal(barrier, inc=1, device_id={"slab": slab_peer(step)}, device_id_type=MESH)
        greeted += 1
    for step in range(1, cores):
        pl.semaphore_signal(barrier, inc=1, device_id={"row": core_peer(step)}, device_id_type=MESH)
        greeted += 1

    def sender(w, k):
        return lax.div(branch_ref[w * slots + k], slots)

    def kth(w, origin, values):
        picks, count = [jnp.int32(0)] * local, jnp.int32(0)
        for k in range(slots):
            hit = sender(w, k) == origin
            picks = [jnp.where(hit & (count == place), values(k), pick) for place, pick in enumerate(picks)]
            count = count + jnp.where(hit, 1, 0)
        return picks

    for copy in own[:3]:
        copy.wait()
    slot_of = list(range(slots))
    if local < slots:
        origins = []
        for step in range(walks):
            target = partner(walk, step, walks)
            picks = kth(target, walk, lambda k: lax.rem(branch_ref[target * slots + k], slots))
            for place, pick in enumerate(picks):
                if step == 0:
                    raw[place, mine] = source[pick]
                else:
                    outgoing[step * local + place] = source[pick]
            origin = target if walks & (walks - 1) == 0 else (walk + walks - step) % walks
            origins.append(origin)
            for place, pick in enumerate(kth(walk, origin, lambda k: k)):
                i = step * local + place
                field_out[i : i + 1, :] = field_in[pl.ds(pick, 1), :]
        for j in range(slots):
            origin, rank, step_of = sender(walk, j), jnp.int32(0), jnp.int32(0)
            for k in range(j):
                rank = rank + jnp.where(sender(walk, k) == origin, 1, 0)
            for step in range(walks):
                step_of = jnp.where(origins[step] == origin, step, step_of)
            slot_of[j] = jnp.minimum(step_of * local + rank, slots - 1)
    else:
        for i in range(slots):
            raw[i, mine] = source[i]
        field_out[...] = field_in[...]
    field[mine] = field_out[...]
    for copy in own[3:]:
        copy.wait()
    pl.semaphore_wait(barrier, greeted)

    def remote(src, dst, send, recv, target):
        return pltpu.make_async_remote_copy(
            src_ref=src, dst_ref=dst, send_sem=send, recv_sem=recv, device_id=target, device_id_type=MESH
        )

    def z_copy(i, step):
        return remote(outgoing.at[i], raw.at[i, mine], z_send.at[i], z_recv.at[i], {"walk": partner(walk, step, walks)})

    def x_copy(i, step):
        return remote(raw.at[i, mine], raw.at[i, mine], x_send.at[step, i], x_recv.at[step, i], {"slab": slab_peer(step)})

    def c_copy(i, hop, step):
        q = slab_source(hop) * cores + core
        return remote(raw.at[i, q], raw.at[i, q], c_send.at[hop, step, i], c_recv.at[hop, step, i], {"row": core_peer(step)})

    def small(src, buf, xs, xr, cs, cr):
        def x(step):
            return remote(src, buf.at[mine], xs.at[step], xr.at[step], {"slab": slab_peer(step)})

        def c(hop, step):
            q = slab_source(hop) * cores + core
            block = src if hop == 0 else buf.at[q]
            return remote(block, buf.at[q], cs.at[hop, step], cr.at[hop, step], {"row": core_peer(step)})

        return x, c

    for i in range(local, slots):
        z_copy(i, i // local).start()
    pairs = [
        small(trial_ref, trial, tx_send, tx_recv, tc_send, tc_recv),
        small(field_out, field, fx_send, fx_recv, fc_send, fc_recv),
    ]
    for x, c in pairs:
        for step in range(1, slabs):
            x(step).start()
        for step in range(1, cores):
            c(0, step).start()
    def spread(i):
        for step in range(1, slabs):
            x_copy(i, step).start()
        for step in range(1, cores):
            c_copy(i, 0, step).start()

    def relay(i):
        for hop in range(1, slabs):
            x_copy(i, hop).wait_recv()
            for step in range(1, cores):
                c_copy(i, hop, step).start()

    def compute(i):
        for hop in range(slabs):
            for step in range(1, cores):
                c_copy(i, hop, step).wait_recv()
        for q in range(slabs * cores):
            column = jnp.transpose(field[q])
            lane = lax.broadcasted_iota(jnp.int32, column.shape, 1)
            scale = jnp.sum(jnp.where(lane == i, column, 0.0), axis=1, keepdims=True)
            prop[q * rows : (q + 1) * rows, :] = (raw[i, q].astype(jnp.float32) * scale).astype(jnp.bfloat16)
        @pl.when(lax.rem(i, cores) == core)
        def _():
            total = dot(trial_t[0], prop[0:rows, :])
            for q in range(1, slabs * cores):
                total += dot(trial_t[q], prop[q * rows : (q + 1) * rows, :])
            inter[i // cores] = total

        half[i] = dot(chol[...], prop[...]).astype(jnp.bfloat16)

    for i in range(local):
        spread(i)
    for x, c in pairs:
        for hop in range(1, slabs):
            x(hop).wait_recv()
            for step in range(1, cores):
                c(hop, step).start()
    for x, c in pairs:
        for hop in range(slabs):
            for step in range(1, cores):
                c(hop, step).wait_recv()

    for q in range(slabs * cores):
        trial_t[q] = jnp.transpose(trial[q].astype(jnp.float32)).astype(jnp.bfloat16)
    share = slots // cores
    line = lax.broadcasted_iota(jnp.int32, (electrons, electrons), 0)
    diagonal = line == lax.broadcasted_iota(jnp.int32, (electrons, electrons), 1)

    def i_copy(i, step):
        place = inverse.at[i]
        return remote(place, place, i_send.at[i // cores, step], i_recv.at[i // cores, step], {"row": core_peer(step)})

    def first_guess(n):
        matrix = inter[n]
        sizes_of = jnp.abs(matrix)
        column_max = jnp.max(jnp.sum(sizes_of, axis=0, keepdims=True), axis=1, keepdims=True)
        row_max = jnp.max(jnp.sum(sizes_of, axis=1, keepdims=True), axis=0, keepdims=True)
        start = jnp.transpose(matrix) / (column_max * row_max)
        stack[0:electrons, :] = start
        stack[electrons:, :] = dot3(matrix, start)

    def finish(i):
        @pl.when(lax.rem(i, cores) != core)
        def _():
            i_copy(i, lax.rem(core + cores - lax.rem(i, cores), cores)).wait_recv()

        contracted = dot(half[i], inverse[i])
        for g in range(vectors):
            block = contracted[g * electrons : (g + 1) * electrons, :]
            traces[i, g : g + 1, :] = jnp.sum(jnp.where(diagonal, block, 0.0), axis=0, keepdims=True)
            squares[i, g : g + 1, :] = jnp.sum(block * jnp.transpose(block), axis=0, keepdims=True)

    ready = cores + 1

    @pl.loop(0, slots + ready + cores + 1)
    def _(i):
        @pl.when((i >= local - 1) & (i < slots - 1))
        def _():
            z_copy(i + 1, 0).wait_recv()
            spread(i + 1)

        @pl.when((i > 1) & (i < slots + 2))
        def _():
            compute(i - 2)

        @pl.when((i > 0) & (i <= slots))
        def _():
            relay(i - 1)

        for part in range(cores):

            @pl.when((i >= ready) & (i < slots + ready) & (lax.rem(i + cores - 1, cores) == part))
            def _():
                n = (i - ready) // cores
                if part == 0:
                    first_guess(n)

                first, middle, last = ITERS * part // cores, EARLY, ITERS * (part + 1) // cores

                @pl.loop(first, max(first, min(middle, last)))
                def _(iteration):
                    both = stack[...]
                    low = both.astype(jnp.bfloat16)
                    stack[...] = 2.0 * both - dot(low, low[electrons:, :])

                @pl.loop(min(last, max(middle, first)), last)
                def _(iteration):
                    both = stack[...]
                    stack[...] = 2.0 * both - dot3(both, both[electrons:, :])

                if part == cores - 1:
                    inverse[n * cores + core] = stack[0:electrons, :].astype(jnp.bfloat16)
                    for step in range(1, cores):
                        i_copy(n * cores + core, step).start()

        @pl.when(i > ready + cores)
        def _():
            finish(i - ready - cores - 1)


    column = lax.broadcasted_iota(jnp.int32, bias_ref.shape, 1)
    for terms, rows_of, result in ((traces, bias_rows, bias_ref), (squares, exch_rows, exch_ref)):
        for j in range(slots):
            block = terms[slot_of[j]]
            for g in range(vectors):
                rows_of[g, j : j + 1, :] = block[g : g + 1, :]
        total = jnp.zeros(result.shape, jnp.float32)
        for g in range(vectors):
            total = jnp.where(column == g, jnp.sum(rows_of[g], axis=1, keepdims=True), total)
        result[...] = total

    for i in range(local, slots):
        z_copy(i, i // local).wait_send()

    @pl.loop(0, slots)
    def _(i):
        for step in range(1, slabs):
            x_copy(i, step).wait_send()
        for hop in range(slabs):
            for step in range(1, cores):
                c_copy(i, hop, step).wait_send()

    for x, c in pairs:
        for step in range(1, slabs):
            x(step).wait_send()
        for hop in range(slabs):
            for step in range(1, cores):
                c(hop, step).wait_send()
    for n in range(share):
        for step in range(1, cores):
            i_copy(n * cores + core, step).wait_send()


def on_device(walkers, trial_orbitals, cholesky, branches, counts, field):
    walks, slabs, cores = lax.axis_size("walk"), lax.axis_size("slab"), lax.axis_size("row")
    walk = lax.axis_index("walk")
    per_device, rows, electrons = walkers.shape
    vectors = cholesky.shape[0]
    capacity = (per_device + walks - 1) // walks
    local = capacity if walks * capacity == per_device else per_device
    if local == per_device:
        sender = branches.reshape(walks, per_device) // per_device
        local_index = branches.reshape(walks, per_device) % per_device
        places = jnp.arange(per_device, dtype=jnp.int32)
        same_sender = sender[:, :, None] == sender[:, None, :]
        rank = jnp.sum(same_sender & (places[None, :] < places[:, None])[None], axis=2)
        ranks = jnp.arange(capacity, dtype=jnp.int32)[None, :, None]
        wanted = (sender[:, None, :] == walk) & (rank[:, None, :] == ranks)
        chosen = jnp.sum(jnp.where(wanted, local_index[:, None, :], 0), axis=2)
        outgoing = jnp.take(walkers, chosen.reshape(-1), axis=0, mode="clip")
        outgoing = outgoing.reshape(walks, capacity, rows, electrons)
        arrived = lax.all_to_all(outgoing, "walk", split_axis=0, concat_axis=0, tiled=True)
        arrived = arrived.reshape(walks * capacity, rows, electrons)
        my_sender = lax.dynamic_index_in_dim(sender, walk, 0, keepdims=False)
        my_rank = lax.dynamic_index_in_dim(rank, walk, 0, keepdims=False)
        walkers = jnp.take(arrived, my_sender * capacity + my_rank, axis=0, mode="clip")
    shards = slabs * cores
    share = per_device // cores
    dma = pltpu.SemaphoreType.DMA
    vmem = pl.BlockSpec(memory_space=pltpu.VMEM)
    bias, exchange = pl.pallas_call(
        functools.partial(kernel, (walks, slabs, cores, per_device, local)),
        out_shape=[jax.ShapeDtypeStruct((per_device, vectors), jnp.float32)] * 2,
        in_specs=[pl.BlockSpec(memory_space=pl.ANY)] * 5,
        out_specs=[vmem] * 2,
        scratch_shapes=[
            pltpu.SMEM(branches.shape, jnp.int32),
            pltpu.VMEM((shards, electrons, rows), jnp.bfloat16),
            pltpu.VMEM((per_device, rows, electrons), jnp.bfloat16),
            pltpu.VMEM((per_device, rows, electrons), jnp.bfloat16),
            pltpu.VMEM((per_device, rows), jnp.float32),
            pltpu.VMEM((per_device, rows), jnp.float32),
            pltpu.VMEM((per_device, vectors, electrons), jnp.float32),
            pltpu.VMEM((per_device, vectors, electrons), jnp.float32),
            pltpu.VMEM((vectors, per_device, electrons), jnp.float32),
            pltpu.VMEM((vectors, per_device, electrons), jnp.float32),
            pltpu.VMEM((per_device, shards, rows, electrons), jnp.bfloat16),
            pltpu.VMEM((shards, rows, electrons), jnp.bfloat16),
            pltpu.VMEM((shards, per_device, rows), jnp.float32),
            pltpu.VMEM((vectors * electrons, shards * rows), jnp.bfloat16),
            pltpu.VMEM((shards * rows, electrons), jnp.bfloat16),
            pltpu.VMEM((per_device, vectors * electrons, electrons), jnp.bfloat16),
            pltpu.VMEM((share, electrons, electrons), jnp.float32),
            pltpu.VMEM((2 * electrons, electrons), jnp.float32),
            pltpu.VMEM((per_device, electrons, electrons), jnp.bfloat16),
            dma((per_device,)), dma((per_device,)),
            dma((slabs, per_device)), dma((slabs, per_device)),
            dma((slabs, cores, per_device)), dma((slabs, cores, per_device)),
            dma((share, cores)), dma((share, cores)),
            dma((slabs,)), dma((slabs,)), dma((slabs, cores)), dma((slabs, cores)),
            dma((slabs,)), dma((slabs,)), dma((slabs, cores)), dma((slabs, cores)),
            dma((5,)),
        ],
        compiler_params=pltpu.CompilerParams(
            collective_id=0, has_side_effects=True, vmem_limit_bytes=63 * 1024 * 1024
        ),
    )(branches, walkers, trial_orbitals, cholesky.reshape(vectors * electrons, shards * rows), field)
    living = (jnp.arange(per_device, dtype=jnp.int32) < counts[0]).astype(jnp.float32)[:, None]
    return bias * living, -0.5 * exchange * living


def solution(mesh):
    return jax.shard_map(
        on_device,
        mesh=mesh,
        in_specs=(
            P(("parts", "walk"), ("slab", "row"), None),
            P(("parts", "slab", "row"), None),
            P(("parts", "slab", "row"), None, None),
            P("parts"),
            P(("parts", "walk")),
            P(("parts", "walk"), ("slab", "row")),
        ),
        out_specs=(P(("parts", "walk"), ("slab", "row")), P(("parts", "walk"), ("slab", "row"))),
        check_vma=False,
    )
```
